512 devices in a mesh: section: 32 (over y_hi, z, core), dp: 16 (over x, y_lo).
Axes of the slice: x: 4, y: 8 (y_hi: 2, y_lo: 4; y = y_hi * 4 + y_lo), z: 8, core: 2. Of those that a mesh axis runs over, the one named last changes fastest.
Arguments:
- section_inputs: bfloat16 [32, 2048, 4096], P('section', 'dp'), may hold values from -6 to 6
- norm_gain: bfloat16 [32, 4096], P('section'), may hold values from 0.5 to 1.5
- down_proj: bfloat16 [32, 4096, 256], P('section', 'dp'), may hold values from -0.09375 to 0.09375
- up_proj: bfloat16 [32, 256, 4096], P('section', None, 'dp'), may hold values from -0.1875 to 0.1875
- readout_matrix: bfloat16 [4096, 128], P('dp'), may hold values from -0.09375 to 0.09375
- ground_truth_series: float32 [2048, 128], P('dp'), may hold values from -6 to 6
- valid_len: int32 [128], P('dp'), may hold values from 1 to 16
Outputs:
- input_grads: bfloat16 [32, 2048, 4096], P('section', 'dp')
- down_grads: bfloat16 [32, 4096, 256], P('section', 'dp')
- up_grads: bfloat16 [32, 256, 4096], P('section', None, 'dp')
The draws below stay inside these ranges and needn't reach their ends.
All inputs are finite; a program needn't handle non-finite values.
Results may differ from the reference program's by a relative error of at most 0.035.
Values may be sent and summed in bfloat16 or wider, within the bound.
A program may use at most 64 MiB of HBM per device.

```python
import jax
import jax.numpy as jnp
from jax import lax

EMBED_WIDTH = 4096
LAT = 256
HORIZON_LENGTH = 128
ROWS = 16
SEQUENCE_TOTAL = 2048
MICRO_ALL = 128
N_SECTION = 32


def place_ends(drawn, key, least, top_value):
    extent = drawn.shape
    place = [jax.random.randint(jax.random.fold_in(key, axis), (), 0, extent[axis]) for axis in range(len(extent))]
    drawn = drawn.at[tuple(place)].set(least)
    longest = extent.index(max(extent))
    place[longest] = (place[longest] + 1) % extent[longest]
    return drawn.at[tuple(place)].set(top_value)


def block_scale(stream_key, shape, pieces, low, largest):
    level = 1.0
    for dim, blocks in pieces:
        draws = jax.random.uniform(jax.random.fold_in(jax.random.fold_in(stream_key, 6), dim), (blocks,), jnp.float32, low / len(pieces), largest / len(pieces))
        level = level * jnp.repeat(jnp.exp(draws), shape[dim] // blocks).reshape((-1,) + (1,) * (len(shape) - 1 - dim))
    return level


def centred(own_key, dims, width, limit, cuts=(), held_as=jnp.bfloat16):
    array = width * jax.random.normal(own_key, dims, jnp.float32)
    if cuts:
        array = array * block_scale(own_key, dims, cuts, -0.22, 0.18)
    return jnp.clip(array, -limit, limit).astype(held_as)


def setup_inputs(seed: int = 0) -> dict:
    splits = jax.random.split(jax.random.key(seed), 8)
    section_inputs = centred(splits[0], (N_SECTION, SEQUENCE_TOTAL, EMBED_WIDTH), 1.0, 6.0, ((0, 32), (1, 16)))
    norm_gain = jnp.clip(1.0 + 0.1 * jax.random.normal(splits[1], (N_SECTION, EMBED_WIDTH), jnp.float32), 0.5, 1.5).astype(jnp.bfloat16)
    down_proj = centred(splits[2], (N_SECTION, EMBED_WIDTH, LAT), EMBED_WIDTH ** -0.5, 0.09375, ((0, 32), (1, 16)))
    up_proj = centred(splits[3], (N_SECTION, LAT, EMBED_WIDTH), (4 * LAT) ** -0.5, 0.1875, ((0, 32), (2, 16)))
    readout_matrix = centred(splits[4], (EMBED_WIDTH, HORIZON_LENGTH), EMBED_WIDTH ** -0.5, 0.09375, ((0, 16),))
    ground_truth_series = centred(splits[5], (SEQUENCE_TOTAL, HORIZON_LENGTH), 1.0, 6.0, ((0, 16),), jnp.float32)
    valid_len = place_ends(jax.random.randint(splits[6], (MICRO_ALL,), 1, ROWS + 1), jax.random.fold_in(splits[6], 1), 1, ROWS).astype(jnp.int32)
    return {"section_inputs": section_inputs, "norm_gain": norm_gain, "down_proj": down_proj, "up_proj": up_proj, "readout_matrix": readout_matrix, "ground_truth_series": ground_truth_series, "valid_len": valid_len}


EPSILON = 1e-05

def normalize(inputs, gain_row):
    values = inputs.astype(jnp.float32)
    inverse = lax.rsqrt(lax.optimization_barrier(jnp.mean(values * values, axis=-1, keepdims=True)) + EPSILON)
    unit = values * inverse
    normed = (unit * gain_row.astype(jnp.float32)).astype(jnp.bfloat16)
    return (inverse, unit, normed)

def multiply_trailing_factor(left, right):
    return lax.dot_general(left, right, (((1,), (1,)), ((), ())), preferred_element_type=jnp.float32)

def contract_rows(left, right):
    return lax.dot_general(left, right, (((0,), (0,)), ((), ())), preferred_element_type=jnp.float32)

def block_backward(inverse, unit, latent, gain_row, down_full, up_full, arriving_gradient):
    sigmoid = jax.nn.sigmoid(latent)
    hidden_grad = multiply_trailing_factor(arriving_gradient, up_full)
    latent_grad = (hidden_grad * sigmoid * (1.0 + latent * (1.0 - sigmoid))).astype(jnp.bfloat16)
    scaled = multiply_trailing_factor(latent_grad, down_full) * gain_row.astype(jnp.float32)
    inputs_grad = arriving_gradient.astype(jnp.float32) + inverse * (scaled - unit * lax.optimization_barrier(jnp.mean(scaled * unit, axis=-1, keepdims=True)))
    return (inputs_grad.astype(jnp.bfloat16), latent_grad)

def reference(section_inputs, norm_gain, down_proj, up_proj, readout_matrix, ground_truth_series, valid_len):
    positions = jnp.arange(SEQUENCE_TOTAL)
    micro_ids = positions // ROWS
    offsets = positions % ROWS
    observed_entry_indicator = (offsets < valid_len[micro_ids]).astype(jnp.float32)
    last = N_SECTION - 1
    inverse, unit, normed = normalize(section_inputs[last], norm_gain[last])
    latent = jnp.dot(normed, down_proj[last], preferred_element_type=jnp.float32)
    activated = jax.nn.silu(latent).astype(jnp.bfloat16)
    adapter_output = (section_inputs[last].astype(jnp.float32) + jnp.dot(activated, up_proj[last], preferred_element_type=jnp.float32)).astype(jnp.bfloat16)
    estimated_horizon = jnp.dot(adapter_output, readout_matrix, preferred_element_type=jnp.float32)
    prediction_discrepancy = (observed_entry_indicator[:, None] * (estimated_horizon - ground_truth_series)).astype(jnp.bfloat16)
    arriving_gradient = multiply_trailing_factor(prediction_discrepancy, readout_matrix).astype(jnp.bfloat16)
    input_list = []
    down_list = []
    up_list = []
    for index in range(N_SECTION - 1, -1, -1):
        inverse, unit, normed = normalize(section_inputs[index], norm_gain[index])
        latent = jnp.dot(normed, down_proj[index], preferred_element_type=jnp.float32)
        activated = jax.nn.silu(latent).astype(jnp.bfloat16)
        inputs_grad, latent_grad = block_backward(inverse, unit, latent, norm_gain[index], down_proj[index], up_proj[index], arriving_gradient)
        down_list.append(contract_rows(normed, latent_grad).astype(jnp.bfloat16))
        up_list.append(contract_rows(activated, arriving_gradient).astype(jnp.bfloat16))
        input_list.append(inputs_grad)
        arriving_gradient = inputs_grad
    return (jnp.stack(input_list[::-1]), jnp.stack(down_list[::-1]), jnp.stack(up_list[::-1]))
```

```python
import functools

import jax
import jax.numpy as jnp
from jax import lax
from jax.experimental import pallas as pl
from jax.experimental.pallas import tpu as pltpu
from jax.sharding import PartitionSpec as P

EPSILON = 1e-05
MESH = pl.DeviceIdType.MESH
F32 = jnp.float32
BF16 = jnp.bfloat16
LINE = 4


def matmul(left, right):
    return jnp.dot(left, right, preferred_element_type=F32)


def matmul_nt(left, right):
    return lax.dot_general(left, right, (((1,), (1,)), ((), ())), preferred_element_type=F32)


def matmul_tn(left, right):
    return lax.dot_general(left, right, (((0,), (0,)), ((), ())), preferred_element_type=F32)


def copy_to(src, dst, send, recv, dev):
    return pltpu.make_async_remote_copy(
        src_ref=src, dst_ref=dst, send_sem=send, recv_sem=recv, device_id=dev, device_id_type=MESH
    )


def kernel(
    ndp,
    nsec,
    x_ref,
    gain_ref,
    down_ref,
    up_ref,
    ro_ref,
    gt_ref,
    vl_ref,
    out_ref,
    dg_ref,
    ug_ref,
    wd,
    wu,
    ro,
    normed,
    ncols,
    act,
    lat,
    dsil,
    inv,
    inc,
    lg,
    cot,
    outp,
    w_send,
    w_recv,
    ro_send,
    ro_recv,
    n_send,
    n_recv,
    a_send,
    a_recv,
    c_send,
    c_recv,
    l_send,
    l_recv,
    r_send,
    r_recv,
    own_sem,
):
    nmb, rows, width = inc.shape
    ntok = nmb * rows
    blk = wd.shape[1]
    latw = wd.shape[2]
    sec = lax.axis_index("section")
    me = lax.axis_index("dp")
    ncol = ndp // LINE
    mx = me // LINE
    my = me % LINE
    last = nsec - 1

    def at(xx, yy):
        return {"dp": (xx % ncol) * LINE + yy % LINE}

    def peer(j):
        return (me + j) % ndp

    barrier = pltpu.get_barrier_semaphore()

    def greet(j, c):
        pl.semaphore_signal(barrier, inc=1, device_id={"dp": peer(j)}, device_id_type=MESH)
        return c

    lax.fori_loop(1, ndp, greet, 0)

    @pl.when(sec > 0)
    def _():
        pl.semaphore_signal(barrier, inc=1, device_id={"section": sec - 1}, device_id_type=MESH)

    @pl.when(sec < last)
    def _():
        pl.semaphore_signal(barrier, inc=1, device_id={"section": sec + 1}, device_id_type=MESH)

    wd[me] = down_ref[...].T
    wu[me] = up_ref[...].T
    ro[me] = ro_ref[...]

    @pl.when((sec > 0) & (sec < last))
    def _():
        pl.semaphore_wait(barrier, ndp + 1)

    @pl.when((sec == 0) | (sec == last))
    def _():
        pl.semaphore_wait(barrier, ndp)

    pieces = (wd, wu)

    def send_block(e, k, dev):
        copy_to(pieces[k].at[e], pieces[k].at[e], w_send, w_recv.at[k, e], dev).start()

    def wait_block(e, k):
        copy_to(pieces[k].at[e], pieces[k].at[e], w_send, w_recv.at[k, e], at(mx, my)).wait_recv()

    for k in (0, 1):
        send_block(me, k, at(mx + 1, my))
        send_block(me, k, at(mx + ncol - 1, my))
        for j in range(1, LINE):
            send_block(me, k, at(mx, my + j))

    @pl.when(sec == last)
    def _():
        def send_ro(j, c):
            copy_to(ro.at[me], ro.at[me], ro_send, ro_recv, {"dp": peer(j)}).start()
            return c

        lax.fori_loop(1, ndp, send_ro, 0)

    gain = gain_ref[...].astype(F32)
    values = x_ref[...].astype(F32)
    inverse = lax.rsqrt(jnp.mean(values * values, axis=-1, keepdims=True) + EPSILON)
    inv[...] = jnp.broadcast_to(inverse, inv.shape)
    for b in range(ndp):
        cols = slice(b * blk, (b + 1) * blk)
        unit = x_ref[:, cols].astype(F32) * inverse
        normed[b] = (unit * gain[:, cols]).astype(BF16)

    for j in range(1, LINE):
        e = mx * LINE + (my + j) % LINE
        for k in (0, 1):
            wait_block(e, k)
            send_block(e, k, at(mx + 1, my))
            send_block(e, k, at(mx + ncol - 1, my))
    for j in range(LINE):
        e_left = ((mx + ncol - 1) % ncol) * LINE + (my + j) % LINE
        e_right = ((mx + 1) % ncol) * LINE + (my + j) % LINE
        wait_block(e_left, 0)
        send_block(e_left, 0, at(mx + 1, my))
        wait_block(e_right, 1)
        send_block(e_right, 1, at(mx + ncol - 1, my))
    for j in range(LINE):
        e_left = ((mx + ncol - 1) % ncol) * LINE + (my + j) % LINE
        e_right = ((mx + 1) % ncol) * LINE + (my + j) % LINE
        e_far = ((mx + 2) % ncol) * LINE + (my + j) % LINE
        wait_block(e_left, 1)
        wait_block(e_right, 0)
        wait_block(e_far, 0)
        wait_block(e_far, 1)

    def latent_step(b, acc):
        return acc + matmul_nt(normed[b], wd[b])

    latent = lax.fori_loop(0, ndp, latent_step, jnp.zeros((ntok, latw), F32))
    lat[...] = latent
    sigmoid = jax.nn.sigmoid(latent)
    activated = (latent * sigmoid).astype(BF16)
    act[me] = activated
    dsil[...] = sigmoid * (1.0 + latent * (1.0 - sigmoid))

    @pl.when(sec == last)
    def _():
        copy_to(ro.at[pl.ds(0, ndp - 1)], ro.at[pl.ds(0, ndp - 1)], ro_send, ro_recv, at(mx, my)).wait_recv()
        hidden = act[me]
        est = jnp.zeros((ntok, ro.shape[2]), F32)
        for b in range(ndp):
            cols = slice(b * blk, (b + 1) * blk)
            adapter = x_ref[:, cols].astype(F32) + matmul_nt(hidden, wu[b])
            est = est + matmul(adapter.astype(BF16), ro[b])
        diff = est - gt_ref[...]
        offset = lax.broadcasted_iota(jnp.int32, (rows, diff.shape[1]), 0)
        errs = []
        for m in range(nmb):
            mask = jnp.where(offset < vl_ref[m], 1.0, 0.0)
            errs.append(mask * diff[m * rows : (m + 1) * rows])
        error = jnp.concatenate(errs, axis=0).astype(BF16)
        for b in range(ndp):
            cols = slice(b * blk, (b + 1) * blk)
            top = matmul_nt(error, ro[b]).astype(BF16)
            inc[:, :, cols] = top.reshape(nmb, rows, blk)

    def send_early(j, c):
        p = peer(j)
        copy_to(act.at[me], act.at[me], a_send, a_recv, {"dp": p}).start()
        copy_to(normed.at[p], ncols.at[me], n_send, n_recv, {"dp": p}).start()
        return c

    lax.fori_loop(1, ndp, send_early, 0)
    ncols[me] = normed[me]

    def relay_copy(m):
        return copy_to(outp.at[m], inc.at[m], r_send.at[m], r_recv.at[m], {"section": (sec + last) % nsec})

    def step(m, c):
        @pl.when(sec < last)
        def _():
            relay_copy(m).wait_recv()

        tok = pl.ds(pl.multiple_of(m * rows, rows), rows)
        h = jnp.zeros((rows, latw), F32)
        for b in range(ndp):
            h = h + matmul(inc[m, :, b * blk : (b + 1) * blk], wu[b])
        latent_grad = (h * dsil[tok, :]).astype(BF16)
        lg[me, m] = latent_grad
        iv = inv[tok, 0:1]
        mean = jnp.sum(latent_grad.astype(F32) * lat[tok, :], axis=-1, keepdims=True) * (1.0 / width)
        for b in range(ndp):
            cols = slice(b * blk, (b + 1) * blk)
            scaled = matmul(latent_grad, wd[b]) * gain_ref[:, cols].astype(F32)
            unit = x_ref[tok, cols].astype(F32) * iv
            g = inc[m, :, cols].astype(F32) + iv * (scaled - unit * mean)
            outp[m, :, cols] = g.astype(BF16)

        @pl.when(sec > 0)
        def _():
            relay_copy(m).start()

        return c

    half = nmb // 2
    own_cols = pl.ds(pl.multiple_of(me * blk, blk), blk)
    for lo, hi in ((0, half), (half, nmb)):
        lax.fori_loop(lo, hi, step, 0)
        part = pl.ds(lo, hi - lo)

        def send_late(j, c, part=part):
            p = peer(j)
            p_cols = pl.ds(pl.multiple_of(p * blk, blk), blk)
            copy_to(inc.at[part, :, p_cols], cot.at[me, part], c_send, c_recv, {"dp": p}).start()
            copy_to(lg.at[me, part], lg.at[me, part], l_send, l_recv, {"dp": p}).start()
            return c

        lax.fori_loop(1, ndp, send_late, 0)
    own = pltpu.make_async_copy(inc.at[:, :, own_cols], cot.at[me], own_sem)
    own.start()
    out_ref[...] = outp[...].reshape(ntok, width)
    own.wait()

    others = pl.ds(0, ndp - 1)
    copy_to(act.at[others], act.at[others], a_send, a_recv, at(mx, my)).wait_recv()
    copy_to(ncols.at[others], ncols.at[others], n_send, n_recv, at(mx, my)).wait_recv()
    copy_to(cot.at[others], cot.at[others], c_send, c_recv, at(mx, my)).wait_recv()
    copy_to(lg.at[others], lg.at[others], l_send, l_recv, at(mx, my)).wait_recv()
    ug = matmul_tn(act[...].reshape(ndp * ntok, latw), cot[...].reshape(ndp * ntok, blk))
    ug_ref[...] = ug.astype(BF16)
    dg = matmul_tn(ncols[...].reshape(ndp * ntok, blk), lg[...].reshape(ndp * ntok, latw))
    dg_ref[...] = dg.astype(BF16)

    for k in (0, 1):
        copy_to(pieces[k].at[others], pieces[k].at[others], w_send, w_recv.at[k, 0], at(mx, my)).wait_send()

    @pl.when(sec == last)
    def _():
        copy_to(ro.at[others], ro.at[others], ro_send, ro_recv, at(mx, my)).wait_send()

    copy_to(act.at[others], act.at[others], a_send, a_recv, at(mx, my)).wait_send()
    copy_to(ncols.at[others], ncols.at[others], n_send, n_recv, at(mx, my)).wait_send()
    copy_to(cot.at[others], cot.at[others], c_send, c_recv, at(mx, my)).wait_send()
    copy_to(lg.at[others], lg.at[others], l_send, l_recv, at(mx, my)).wait_send()

    @pl.when(sec > 0)
    def _():
        def left(m, c):
            relay_copy(m).wait_send()
            return c

        lax.fori_loop(0, nmb, left, 0)


def per_device(
    ndp, nsec, section_inputs, norm_gain, down_proj, up_proj, readout_matrix, ground_truth_series, valid_len
):
    _, ntok, width = section_inputs.shape
    _, blk, latw = down_proj.shape
    horizon = readout_matrix.shape[1]
    nmb = valid_len.shape[0]
    rows = ntok // nmb
    vmem = pl.BlockSpec(memory_space=pltpu.VMEM)
    dma = pltpu.SemaphoreType.DMA
    grads, dg, ug = pl.pallas_call(
        functools.partial(kernel, ndp, nsec),
        name="relay",
        out_shape=(
            jax.ShapeDtypeStruct((ntok, width), BF16),
            jax.ShapeDtypeStruct((blk, latw), BF16),
            jax.ShapeDtypeStruct((latw, blk), BF16),
        ),
        in_specs=[vmem] * 6 + [pl.BlockSpec(memory_space=pltpu.SMEM)],
        out_specs=(vmem, vmem, vmem),
        scratch_shapes=[
            pltpu.VMEM((ndp, latw, blk), BF16),
            pltpu.VMEM((ndp, blk, latw), BF16),
            pltpu.VMEM((ndp, blk, horizon), BF16),
            pltpu.VMEM((ndp, ntok, blk), BF16),
            pltpu.VMEM((ndp, ntok, blk), BF16),
            pltpu.VMEM((ndp, ntok, latw), BF16),
            pltpu.VMEM((ntok, latw), F32),
            pltpu.VMEM((ntok, latw), F32),
            pltpu.VMEM((ntok, 128), F32),
            pltpu.VMEM((nmb, rows, width), BF16),
            pltpu.VMEM((ndp, nmb, rows, latw), BF16),
            pltpu.VMEM((ndp, nmb, rows, blk), BF16),
            pltpu.VMEM((nmb, rows, width), BF16),
            dma,
            dma((2, ndp)),
            dma,
            dma,
            dma,
            dma,
            dma,
            dma,
            dma,
            dma,
            dma,
            dma,
            dma((nmb,)),
            dma((nmb,)),
            dma,
        ],
        compiler_params=pltpu.CompilerParams(collective_id=0, has_side_effects=True),
    )(
        section_inputs[0],
        norm_gain,
        down_proj[0],
        up_proj[0],
        readout_matrix,
        ground_truth_series,
        valid_len,
    )
    return grads[None], dg[None], ug[None]


def solution(mesh):
    placed = (
        P("section", "dp", None),
        P("section", None),
        P("section", "dp", None),
        P("section", None, "dp"),
        P("dp", None),
        P("dp", None),
        P("dp"),
    )
    return jax.shard_map(
        functools.partial(per_device, mesh.shape["dp"], mesh.shape["section"]),
        mesh=mesh,
        in_specs=placed,
        out_specs=(P("section", "dp", None), P("section", "dp", None), P("section", None, "dp")),
        check_vma=False,
    )
```

```python
import functools

import jax
import jax.numpy as jnp
from jax import lax
from jax.experimental import pallas as pl
from jax.experimental.pallas import tpu as pltpu
from jax.sharding import PartitionSpec as P

EPSILON = 1e-05
MESH = pl.DeviceIdType.MESH
F32 = jnp.float32
BF16 = jnp.bfloat16
LINE = 4
GROUP = 2
TOP = 8
SPLIT = 4
COT_GROUPS = 2


def matmul(left, right):
    return jnp.dot(left, right, preferred_element_type=F32)


def matmul_nt(left, right):
    return lax.dot_general(left, right, (((1,), (1,)), ((), ())), preferred_element_type=F32)


def matmul_tn(left, right):
    return lax.dot_general(left, right, (((0,), (0,)), ((), ())), preferred_element_type=F32)


def copy_to(src, dst, send, recv, dev):
    return pltpu.make_async_remote_copy(
        src_ref=src, dst_ref=dst, send_sem=send, recv_sem=recv, device_id=dev, device_id_type=MESH
    )


def kernel(
    ndp,
    nsec,
    x_ref,
    gain_ref,
    down_ref,
    up_ref,
    ro_ref,
    gt_ref,
    vl_ref,
    out_ref,
    dg_ref,
    ug_ref,
    wd,
    wu,
    ro,
    normed,
    ncols,
    act,
    lat,
    dsil,
    inv,
    inc,
    lg,
    cot,
    outp,
    w_send,
    w_recv,
    ro_send,
    ro_recv,
    n_send,
    n_recv,
    a_send,
    a_recv,
    c_send,
    c_recv,
    l_send,
    l_recv,
    r_send,
    r_recv,
    own_sem,
    clear,
):
    nmb, rows, width = inc.shape
    ntok = nmb * rows
    blk = wd.shape[1]
    latw = wd.shape[2]
    sec = lax.axis_index("section")
    me = lax.axis_index("dp")
    ncol = ndp // LINE
    mx = me // LINE
    my = me % LINE
    last = nsec - 1

    def at(xx, yy):
        return {"dp": (xx % ncol) * LINE + yy % LINE}

    def peer(j):
        return (me + j) % ndp

    barrier = pltpu.get_barrier_semaphore()

    def greet(j, c):
        pl.semaphore_signal(barrier, inc=1, device_id={"dp": peer(j)}, device_id_type=MESH)
        return c

    lax.fori_loop(1, ndp, greet, 0)

    @pl.when(sec > 0)
    def _():
        pl.semaphore_signal(barrier, inc=1, device_id={"section": sec - 1}, device_id_type=MESH)

    @pl.when(sec < last)
    def _():
        pl.semaphore_signal(barrier, inc=1, device_id={"section": sec + 1}, device_id_type=MESH)

    wd[me] = down_ref[...].T
    wu[me] = up_ref[...].T
    ro[me] = ro_ref[...]

    @pl.when((sec > 0) & (sec < last))
    def _():
        pl.semaphore_wait(barrier, ndp + 1)

    @pl.when((sec == 0) | (sec == last))
    def _():
        pl.semaphore_wait(barrier, ndp)

    pieces = (wd, wu)

    def send_block(e, k, dev):
        copy_to(pieces[k].at[e], pieces[k].at[e], w_send, w_recv.at[k, e], dev).start()

    def wait_block(e, k):
        copy_to(pieces[k].at[e], pieces[k].at[e], w_send, w_recv.at[k, e], at(mx, my)).wait_recv()

    left, right = at(mx + ncol - 1, my), at(mx + 1, my)
    order = (my, 1 + my % 2, (my * 3 + 2) % 5, 3 * (1 - my // 2))

    def column(shift, row):
        return ((mx + shift + ncol) % ncol) * LINE + row

    even = sec % 2 == 0


    for k in (0, 1):
        send_block(me, k, left)
        send_block(me, k, right)
        for row in order[1:]:
            send_block(me, k, at(mx, row))

    @pl.when(sec == last)
    def _():
        def send_ro(j, c):
            copy_to(ro.at[me], ro.at[me], ro_send, ro_recv, {"dp": peer(j)}).start()
            return c

        lax.fori_loop(1, ndp, send_ro, 0)

    gain = gain_ref[...].astype(F32)
    values = x_ref[...].astype(F32)
    inverse = lax.rsqrt(jnp.mean(values * values, axis=-1, keepdims=True) + EPSILON)
    inv[...] = jnp.broadcast_to(inverse, inv.shape)
    for b in range(ndp):
        cols = slice(b * blk, (b + 1) * blk)
        unit = x_ref[:, cols].astype(F32) * inverse
        normed[b] = (unit * gain[:, cols]).astype(BF16)

    for i in range(1, LINE + 1):
        if i < LINE:
            for k in (0, 1):
                e = column(0, order[i])
                wait_block(e, k)
                send_block(e, k, left)
                send_block(e, k, right)
        e = column(-1, order[i - 1])
        wait_block(e, 0)
        send_block(e, 0, right)
        e = column(1, order[i - 1])
        wait_block(e, 1)
        send_block(e, 1, left)
    for row in order:
        wait_block(column(-1, row), 1)
        wait_block(column(1, row), 0)
        wait_block(column(2, row), 0)
        wait_block(column(2, row), 1)


    def latent_step(b, acc):
        return acc + matmul_nt(normed[b], wd[b])

    latent = lax.fori_loop(0, ndp, latent_step, jnp.zeros((ntok, latw), F32))
    lat[...] = latent
    sigmoid = jax.nn.sigmoid(latent)
    activated = (latent * sigmoid).astype(BF16)
    act[me] = activated
    dsil[...] = sigmoid * (1.0 + latent * (1.0 - sigmoid))

    @pl.when(sec == last)
    def _():
        copy_to(ro.at[pl.ds(0, ndp - 1)], ro.at[pl.ds(0, ndp - 1)], ro_send, ro_recv, at(mx, my)).wait_recv()
        hidden = act[me]
        est = jnp.zeros((ntok, ro.shape[2]), F32)
        for b in range(ndp):
            cols = slice(b * blk, (b + 1) * blk)
            adapter = x_ref[:, cols].astype(F32) + matmul_nt(hidden, wu[b])
            est = est + matmul(adapter.astype(BF16), ro[b])
        diff = est - gt_ref[...]
        offset = lax.broadcasted_iota(jnp.int32, (rows, diff.shape[1]), 0)
        errs = []
        for m in range(nmb):
            mask = jnp.where(offset < vl_ref[m], 1.0, 0.0)
            errs.append(mask * diff[m * rows : (m + 1) * rows])
        error = jnp.concatenate(errs, axis=0).astype(BF16)
        for b in range(ndp):
            cols = slice(b * blk, (b + 1) * blk)
            top = matmul_nt(error, ro[b]).astype(BF16)
            inc[:, :, cols] = top.reshape(nmb, rows, blk)

    def send_early(j, c):
        p = peer(j)
        copy_to(act.at[me], act.at[me], a_send, a_recv, {"dp": p}).start()
        copy_to(normed.at[p], ncols.at[me], n_send, n_recv, {"dp": p}).start()
        return c

    @pl.when(even & (sec < nsec - TOP))
    def _():
        pl.semaphore_signal(clear, inc=1, device_id={"section": sec + 1}, device_id_type=MESH)

    @pl.when(jnp.logical_not(even) & (sec < nsec - TOP))
    def _():
        pl.semaphore_wait(clear, 1)

    @pl.when(sec < nsec - TOP)
    def _():
        lax.fori_loop(1, ndp, send_early, 0)

    ncols[me] = normed[me]

    below = {"section": (sec + last) % nsec}
    per = ndp // SPLIT

    def relay_copy(m, q):
        cols = slice(q * per * blk, (q + 1) * per * blk)
        return copy_to(outp.at[m, :, cols], inc.at[m, :, cols], r_send.at[m, q], r_recv.at[m, q], below)

    def step(m, c):
        tok = pl.ds(pl.multiple_of(m * rows, rows), rows)
        h = jnp.zeros((rows, latw), F32)
        for q in range(SPLIT):

            @pl.when(sec < last)
            def _(q=q):
                relay_copy(m, q).wait_recv()

            for b in range(q * per, (q + 1) * per):
                h = h + matmul(inc[m, :, b * blk : (b + 1) * blk], wu[b])
        latent_grad = (h * dsil[tok, :]).astype(BF16)
        lg[me, m] = latent_grad
        iv = inv[tok, 0:1]
        mean = jnp.sum(latent_grad.astype(F32) * lat[tok, :], axis=-1, keepdims=True) * (1.0 / width)
        for q in range(SPLIT):
            for b in range(q * per, (q + 1) * per):
                cols = slice(b * blk, (b + 1) * blk)
                scaled = matmul(latent_grad, wd[b]) * gain_ref[:, cols].astype(F32)
                unit = x_ref[tok, cols].astype(F32) * iv
                g = inc[m, :, cols].astype(F32) + iv * (scaled - unit * mean)
                outp[m, :, cols] = g.astype(BF16)

            @pl.when(sec > 0)
            def _(q=q):
                relay_copy(m, q).start()

        return c

    own_cols = pl.ds(pl.multiple_of(me * blk, blk), blk)

    def send_lg(e, g, dev):
        part = pl.ds(g * GROUP, GROUP)
        copy_to(lg.at[e, part], lg.at[e, part], l_send, l_recv.at[e, g], dev).start()

    def wait_lg(e, g):
        part = pl.ds(g * GROUP, GROUP)
        copy_to(lg.at[e, part], lg.at[e, part], l_send, l_recv.at[e, g], left).wait_recv()

    def pass_on(g):
        @pl.when(g < groups)
        def _():
            send_lg(me, g, left)
            send_lg(me, g, right)
            for row in order[1:]:
                send_lg(me, g, at(mx, row))
        @pl.when((g < groups) & (g % COT_GROUPS == COT_GROUPS - 1))
        def _():
            part = pl.ds((g + 1 - COT_GROUPS) * GROUP, GROUP * COT_GROUPS)

            def send_cot(j, c):
                p = peer(j)
                p_cols = pl.ds(pl.multiple_of(p * blk, blk), blk)
                copy_to(inc.at[part, :, p_cols], cot.at[me, part], c_send, c_recv, {"dp": p}).start()
                return c

            lax.fori_loop(1, ndp, send_cot, 0)

        @pl.when((g >= 1) & (g <= groups))
        def _():
            for row in order[1:]:
                wait_lg(column(0, row), g - 1)
                send_lg(column(0, row), g - 1, left)
                send_lg(column(0, row), g - 1, right)

        @pl.when(g >= 2)
        def _():
            for n, row in enumerate(order):
                near = 1 if n % 2 else -1
                e = column(near, row)
                wait_lg(e, g - 2)
                send_lg(e, g - 2, left if n % 2 else right)

    groups = nmb // GROUP

    def stretch(g, c):
        lax.fori_loop(g * GROUP, (g + 1) * GROUP, step, 0)
        pass_on(g)
        return c

    lax.fori_loop(0, groups, stretch, 0)
    pass_on(groups)
    pass_on(groups + 1)

    @pl.when(sec >= nsec - TOP)
    def _():
        lax.fori_loop(1, ndp, send_early, 0)

    own = pltpu.make_async_copy(inc.at[:, :, own_cols], cot.at[me], own_sem)
    own.start()
    out_ref[...] = outp[...].reshape(ntok, width)
    own.wait()

    others = pl.ds(0, ndp - 1)
    copy_to(act.at[others], act.at[others], a_send, a_recv, at(mx, my)).wait_recv()
    copy_to(ncols.at[others], ncols.at[others], n_send, n_recv, at(mx, my)).wait_recv()
    copy_to(cot.at[others], cot.at[others], c_send, c_recv, at(mx, my)).wait_recv()

    def last_lg(g, c):
        for n, row in enumerate(order):
            wait_lg(column(-1 if n % 2 else 1, row), g)
            wait_lg(column(2, row), g)
        return c

    lax.fori_loop(0, groups, last_lg, 0)
    ug = matmul_tn(act[...].reshape(ndp * ntok, latw), cot[...].reshape(ndp * ntok, blk))
    ug_ref[...] = ug.astype(BF16)
    dg = matmul_tn(ncols[...].reshape(ndp * ntok, blk), lg[...].reshape(ndp * ntok, latw))
    dg_ref[...] = dg.astype(BF16)

    for k in (0, 1):
        copy_to(pieces[k].at[others], pieces[k].at[others], w_send, w_recv.at[k, 0], at(mx, my)).wait_send()

    @pl.when(sec == last)
    def _():
        copy_to(ro.at[others], ro.at[others], ro_send, ro_recv, at(mx, my)).wait_send()

    copy_to(act.at[others], act.at[others], a_send, a_recv, at(mx, my)).wait_send()
    copy_to(ncols.at[others], ncols.at[others], n_send, n_recv, at(mx, my)).wait_send()
    copy_to(cot.at[others], cot.at[others], c_send, c_recv, at(mx, my)).wait_send()
    copy_to(lg.at[others], lg.at[others], l_send, l_recv.at[0, 0], left).wait_send()

    @pl.when(sec > 0)
    def _():
        def gone(m, c):
            for q in range(SPLIT):
                relay_copy(m, q).wait_send()
            return c

        lax.fori_loop(0, nmb, gone, 0)


def per_device(
    ndp, nsec, section_inputs, norm_gain, down_proj, up_proj, readout_matrix, ground_truth_series, valid_len
):
    _, ntok, width = section_inputs.shape
    _, blk, latw = down_proj.shape
    horizon = readout_matrix.shape[1]
    nmb = valid_len.shape[0]
    rows = ntok // nmb
    vmem = pl.BlockSpec(memory_space=pltpu.VMEM)
    dma = pltpu.SemaphoreType.DMA
    grads, dg, ug = pl.pallas_call(
        functools.partial(kernel, ndp, nsec),
        name="relay",
        out_shape=(
            jax.ShapeDtypeStruct((ntok, width), BF16),
            jax.ShapeDtypeStruct((blk, latw), BF16),
            jax.ShapeDtypeStruct((latw, blk), BF16),
        ),
        in_specs=[vmem] * 6 + [pl.BlockSpec(memory_space=pltpu.SMEM)],
        out_specs=(vmem, vmem, vmem),
        scratch_shapes=[
            pltpu.VMEM((ndp, latw, blk), BF16),
            pltpu.VMEM((ndp, blk, latw), BF16),
            pltpu.VMEM((ndp, blk, horizon), BF16),
            pltpu.VMEM((ndp, ntok, blk), BF16),
            pltpu.VMEM((ndp, ntok, blk), BF16),
            pltpu.VMEM((ndp, ntok, latw), BF16),
            pltpu.VMEM((ntok, latw), F32),
            pltpu.VMEM((ntok, latw), F32),
            pltpu.VMEM((ntok, 128), F32),
            pltpu.VMEM((nmb, rows, width), BF16),
            pltpu.VMEM((ndp, nmb, rows, latw), BF16),
            pltpu.VMEM((ndp, nmb, rows, blk), BF16),
            pltpu.VMEM((nmb, rows, width), BF16),
            dma,
            dma((2, ndp)),
            dma,
            dma,
            dma,
            dma,
            dma,
            dma,
            dma,
            dma,
            dma,
            dma((ndp, nmb // GROUP)),
            dma((nmb, SPLIT)),
            dma((nmb, SPLIT)),
            dma,
            pltpu.SemaphoreType.REGULAR,
        ],
        compiler_params=pltpu.CompilerParams(collective_id=0, has_side_effects=True),
    )(
        section_inputs[0],
        norm_gain,
        down_proj[0],
        up_proj[0],
        readout_matrix,
        ground_truth_series,
        valid_len,
    )
    return grads[None], dg[None], ug[None]


def solution(mesh):
    placed = (
        P("section", "dp", None),
        P("section", None),
        P("section", "dp", None),
        P("section", None, "dp"),
        P("dp", None),
        P("dp", None),
        P("dp"),
    )
    return jax.shard_map(
        functools.partial(per_device, mesh.shape["dp"], mesh.shape["section"]),
        mesh=mesh,
        in_specs=placed,
        out_specs=(P("section", "dp", None), P("section", "dp", None), P("section", None, "dp")),
        check_vma=False,
    )
```

```python
import functools

import jax
import jax.numpy as jnp
from jax import lax
from jax.experimental import pallas as pl
from jax.experimental.pallas import tpu as pltpu
from jax.sharding import PartitionSpec as P

EPSILON = 1e-05
MESH = pl.DeviceIdType.MESH
F32 = jnp.float32
BF16 = jnp.bfloat16
LINE = 4
GROUP = 2
TOP = 8
SPLIT = 4
COT_GROUPS = 2


def matmul(left, right):
    return jnp.dot(left, right, preferred_element_type=F32)


def matmul_nt(left, right):
    return lax.dot_general(left, right, (((1,), (1,)), ((), ())), preferred_element_type=F32)


def matmul_tn(left, right):
    return lax.dot_general(left, right, (((0,), (0,)), ((), ())), preferred_element_type=F32)


def copy_to(src, dst, send, recv, dev):
    return pltpu.make_async_remote_copy(
        src_ref=src, dst_ref=dst, send_sem=send, recv_sem=recv, device_id=dev, device_id_type=MESH
    )


def kernel(
    ndp,
    nsec,
    x_ref,
    gain_ref,
    down_ref,
    up_ref,
    ro_ref,
    gt_ref,
    vl_ref,
    out_ref,
    dg_ref,
    ug_ref,
    wd,
    wu,
    ro,
    normed,
    ncols,
    act,
    lat,
    dsil,
    inv,
    inc,
    lg,
    cot,
    outp,
    est,
    w_send,
    w_recv,
    ro_send,
    ro_recv,
    n_send,
    n_recv,
    a_send,
    a_recv,
    c_send,
    c_recv,
    l_send,
    l_recv,
    r_send,
    r_recv,
    own_sem,
    out_sem,
    clear,
):
    nmb, rows, width = inc.shape
    ntok = nmb * rows
    blk = wd.shape[1]
    latw = wd.shape[2]
    sec = lax.axis_index("section")
    me = lax.axis_index("dp")
    ncol = ndp // LINE
    mx = me // LINE
    my = me % LINE
    last = nsec - 1

    def at(xx, yy):
        return {"dp": (xx % ncol) * LINE + yy % LINE}

    def peer(j):
        return (me + j) % ndp

    barrier = pltpu.get_barrier_semaphore()

    def greet(j, c):
        pl.semaphore_signal(barrier, inc=1, device_id={"dp": peer(j)}, device_id_type=MESH)
        return c

    lax.fori_loop(1, ndp, greet, 0)

    @pl.when(sec > 0)
    def _():
        pl.semaphore_signal(barrier, inc=1, device_id={"section": sec - 1}, device_id_type=MESH)

    @pl.when(sec < last)
    def _():
        pl.semaphore_signal(barrier, inc=1, device_id={"section": sec + 1}, device_id_type=MESH)

    wd[me] = down_ref[...].T
    wu[me] = up_ref[...].T
    ro[me] = ro_ref[...]

    @pl.when((sec > 0) & (sec < last))
    def _():
        pl.semaphore_wait(barrier, ndp + 1)

    @pl.when((sec == 0) | (sec == last))
    def _():
        pl.semaphore_wait(barrier, ndp)

    pieces = (wd, wu)

    def send_block(e, k, dev):
        copy_to(pieces[k].at[e], pieces[k].at[e], w_send, w_recv.at[k, e], dev).start()

    def wait_block(e, k):
        copy_to(pieces[k].at[e], pieces[k].at[e], w_send, w_recv.at[k, e], at(mx, my)).wait_recv()

    left, right = at(mx + ncol - 1, my), at(mx + 1, my)
    order = (my, 1 + my % 2, (my * 3 + 2) % 5, 3 * (1 - my // 2))

    def column(shift, row):
        return ((mx + shift + ncol) % ncol) * LINE + row

    even = sec % 2 == 0


    for k in (0, 1):
        send_block(me, k, left)
        send_block(me, k, right)
        for row in order[1:]:
            send_block(me, k, at(mx, row))

    @pl.when(sec == last)
    def _():
        def send_ro(j, c):
            copy_to(ro.at[me], ro.at[me], ro_send, ro_recv, {"dp": peer(j)}).start()
            return c

        lax.fori_loop(1, ndp, send_ro, 0)

    gain = gain_ref[...].astype(F32)
    values = x_ref[...].astype(F32)
    inverse = lax.rsqrt(jnp.mean(values * values, axis=-1, keepdims=True) + EPSILON)
    inv[...] = jnp.broadcast_to(inverse, inv.shape)
    for b in range(ndp):
        cols = slice(b * blk, (b + 1) * blk)
        unit = x_ref[:, cols].astype(F32) * inverse
        normed[b] = (unit * gain[:, cols]).astype(BF16)

    for k, near, way in ((0, -1, right), (1, 1, left)):
        for i in range(1, LINE + 1):
            if i < LINE:
                e = column(0, order[i])
                wait_block(e, k)
                send_block(e, k, left)
                send_block(e, k, right)
            e = column(near, order[i - 1])
            wait_block(e, k)
            send_block(e, k, way)
    for row in order:
        wait_block(column(1, row), 0)
        wait_block(column(2, row), 0)

    def latent_step(b, acc):
        return acc + matmul_nt(normed[b], wd[b])

    latent = lax.fori_loop(0, ndp, latent_step, jnp.zeros((ntok, latw), F32))
    lat[...] = latent
    sigmoid = jax.nn.sigmoid(latent)
    activated = (latent * sigmoid).astype(BF16)
    act[me] = activated
    dsil[...] = sigmoid * (1.0 + latent * (1.0 - sigmoid))

    def forecast(e, first=False):
        cols = pl.ds(pl.multiple_of(e * blk, blk), blk)
        adapter = x_ref[:, cols].astype(F32) + matmul_nt(act[me], wu[e])
        part = matmul(adapter.astype(BF16), ro[e])
        est[...] = part if first else est[...] + part

    @pl.when(sec == last)
    def _():
        copy_to(ro.at[pl.ds(0, ndp - 1)], ro.at[pl.ds(0, ndp - 1)], ro_send, ro_recv, at(mx, my)).wait_recv()
        forecast(me, True)
        for row in order[1:]:
            forecast(column(0, row))
        for row in order:
            forecast(column(1, row))

    for shift in (-1, 2):
        for row in order:
            wait_block(column(shift, row), 1)

            @pl.when(sec == last)
            def _(shift=shift, row=row):
                forecast(column(shift, row))

    @pl.when(sec == last)
    def _():
        diff = est[...] - gt_ref[...]
        offset = lax.broadcasted_iota(jnp.int32, (rows, diff.shape[1]), 0)
        errs = []
        for m in range(nmb):
            mask = jnp.where(offset < vl_ref[m], 1.0, 0.0)
            errs.append(mask * diff[m * rows : (m + 1) * rows])
        error = jnp.concatenate(errs, axis=0).astype(BF16)
        for b in range(ndp):
            cols = slice(b * blk, (b + 1) * blk)
            top = matmul_nt(error, ro[b]).astype(BF16)
            inc[:, :, cols] = top.reshape(nmb, rows, blk)

    def send_early(j, c):
        p = peer(j)
        copy_to(act.at[me], act.at[me], a_send, a_recv, {"dp": p}).start()
        copy_to(normed.at[p], ncols.at[me], n_send, n_recv, {"dp": p}).start()
        return c

    @pl.when(even & (sec < nsec - TOP))
    def _():
        pl.semaphore_signal(clear, inc=1, device_id={"section": sec + 1}, device_id_type=MESH)

    @pl.when(jnp.logical_not(even) & (sec < nsec - TOP))
    def _():
        pl.semaphore_wait(clear, 1)

    @pl.when(sec < nsec - TOP)
    def _():
        lax.fori_loop(1, ndp, send_early, 0)

    ncols[me] = normed[me]

    below = {"section": (sec + last) % nsec}
    per = ndp // SPLIT

    def relay_copy(m, q):
        cols = slice(q * per * blk, (q + 1) * per * blk)
        return copy_to(outp.at[m, :, cols], inc.at[m, :, cols], r_send.at[m, q], r_recv.at[m, q], below)

    def step(m, c):
        tok = pl.ds(pl.multiple_of(m * rows, rows), rows)
        h = jnp.zeros((rows, latw), F32)
        for q in range(SPLIT):

            @pl.when(sec < last)
            def _(q=q):
                relay_copy(m, q).wait_recv()

            for b in range(q * per, (q + 1) * per):
                h = h + matmul(inc[m, :, b * blk : (b + 1) * blk], wu[b])
        latent_grad = (h * dsil[tok, :]).astype(BF16)
        lg[me, m] = latent_grad
        iv = inv[tok, 0:1]
        mean = jnp.sum(latent_grad.astype(F32) * lat[tok, :], axis=-1, keepdims=True) * (1.0 / width)
        for q in range(SPLIT):
            for b in range(q * per, (q + 1) * per):
                cols = slice(b * blk, (b + 1) * blk)
                scaled = matmul(latent_grad, wd[b]) * gain_ref[:, cols].astype(F32)
                unit = x_ref[tok, cols].astype(F32) * iv
                g = inc[m, :, cols].astype(F32) + iv * (scaled - unit * mean)
                outp[m, :, cols] = g.astype(BF16)

            @pl.when(sec > 0)
            def _(q=q):
                relay_copy(m, q).start()

        return c

    own_cols = pl.ds(pl.multiple_of(me * blk, blk), blk)

    def send_lg(e, g, dev):
        part = pl.ds(g * GROUP, GROUP)
        copy_to(lg.at[e, part], lg.at[e, part], l_send, l_recv.at[e, g], dev).start()

    def wait_lg(e, g):
        part = pl.ds(g * GROUP, GROUP)
        copy_to(lg.at[e, part], lg.at[e, part], l_send, l_recv.at[e, g], left).wait_recv()

    def pass_on(g):
        @pl.when(g < groups)
        def _():
            send_lg(me, g, left)
            send_lg(me, g, right)
            for row in order[1:]:
                send_lg(me, g, at(mx, row))
        @pl.when((g < groups) & (g % COT_GROUPS == COT_GROUPS - 1))
        def _():
            part = pl.ds((g + 1 - COT_GROUPS) * GROUP, GROUP * COT_GROUPS)

            def send_cot(j, c):
                p = peer(j)
                p_cols = pl.ds(pl.multiple_of(p * blk, blk), blk)
                copy_to(inc.at[part, :, p_cols], cot.at[me, part], c_send, c_recv, {"dp": p}).start()
                return c

            lax.fori_loop(1, ndp, send_cot, 0)

        @pl.when((g >= 1) & (g <= groups))
        def _():
            for row in order[1:]:
                wait_lg(column(0, row), g - 1)
                send_lg(column(0, row), g - 1, left)
                send_lg(column(0, row), g - 1, right)

        @pl.when(g >= 2)
        def _():
            for n, row in enumerate(order):
                near = 1 if n % 2 else -1
                e = column(near, row)
                wait_lg(e, g - 2)
                send_lg(e, g - 2, left if n % 2 else right)

    groups = nmb // GROUP

    def stretch(g, c):
        lax.fori_loop(g * GROUP, (g + 1) * GROUP, step, 0)
        part = pl.ds(g * GROUP, GROUP)
        pltpu.make_async_copy(outp.at[part], out_ref.at[part], out_sem).start()
        pass_on(g)
        return c

    lax.fori_loop(0, groups, stretch, 0)
    pass_on(groups)
    pass_on(groups + 1)

    @pl.when(sec >= nsec - TOP)
    def _():
        lax.fori_loop(1, ndp, send_early, 0)

    own = pltpu.make_async_copy(inc.at[:, :, own_cols], cot.at[me], own_sem)
    own.start()
    own.wait()

    others = pl.ds(0, ndp - 1)
    copy_to(act.at[others], act.at[others], a_send, a_recv, at(mx, my)).wait_recv()
    copy_to(ncols.at[others], ncols.at[others], n_send, n_recv, at(mx, my)).wait_recv()
    copy_to(cot.at[others], cot.at[others], c_send, c_recv, at(mx, my)).wait_recv()

    def last_lg(g, c):
        for n, row in enumerate(order):
            wait_lg(column(-1 if n % 2 else 1, row), g)
            wait_lg(column(2, row), g)
        return c

    lax.fori_loop(0, groups, last_lg, 0)
    ug = matmul_tn(act[...].reshape(ndp * ntok, latw), cot[...].reshape(ndp * ntok, blk))
    ug_ref[...] = ug.astype(BF16)
    dg = matmul_tn(ncols[...].reshape(ndp * ntok, blk), lg[...].reshape(ndp * ntok, latw))
    dg_ref[...] = dg.astype(BF16)

    pltpu.make_async_copy(outp, out_ref, out_sem).wait()
    for k in (0, 1):
        copy_to(pieces[k].at[others], pieces[k].at[others], w_send, w_recv.at[k, 0], at(mx, my)).wait_send()

    @pl.when(sec == last)
    def _():
        copy_to(ro.at[others], ro.at[others], ro_send, ro_recv, at(mx, my)).wait_send()

    copy_to(act.at[others], act.at[others], a_send, a_recv, at(mx, my)).wait_send()
    copy_to(ncols.at[others], ncols.at[others], n_send, n_recv, at(mx, my)).wait_send()
    copy_to(cot.at[others], cot.at[others], c_send, c_recv, at(mx, my)).wait_send()
    copy_to(lg.at[others], lg.at[others], l_send, l_recv.at[0, 0], left).wait_send()

    @pl.when(sec > 0)
    def _():
        def gone(m, c):
            for q in range(SPLIT):
                relay_copy(m, q).wait_send()
            return c

        lax.fori_loop(0, nmb, gone, 0)


def hand_over_kernel(pieces, a_in, b_in, c_in, a_out, b_out, c_out, a_buf, b_buf, c_buf, in_sem, out_sem):
    rows = a_buf.shape[0] // pieces
    jobs = [(b_in, b_buf, b_out), (c_in, c_buf, c_out)]
    for i in range(pieces):
        part = pl.ds(i * rows, rows)
        jobs.append((a_in.at[part], a_buf.at[part], a_out.at[part]))
    for i, (src, buf, _) in enumerate(jobs):
        pltpu.make_async_copy(src, buf, in_sem.at[i]).start()
    for i, (src, buf, dst) in enumerate(jobs):
        pltpu.make_async_copy(src, buf, in_sem.at[i]).wait()
        pltpu.make_async_copy(buf, dst, out_sem.at[i]).start()
    for i, (_, buf, dst) in enumerate(jobs):
        pltpu.make_async_copy(buf, dst, out_sem.at[i]).wait()


def hand_over(*arrays, pieces=4):
    anywhere = pl.BlockSpec(memory_space=pl.ANY)
    return pl.pallas_call(
        functools.partial(hand_over_kernel, pieces),
        name="hand_over",
        out_shape=tuple(jax.ShapeDtypeStruct(a.shape, a.dtype) for a in arrays),
        in_specs=[anywhere] * 3,
        out_specs=(anywhere,) * 3,
        scratch_shapes=[pltpu.VMEM(a.shape, a.dtype) for a in arrays]
        + [pltpu.SemaphoreType.DMA((2 + pieces,)), pltpu.SemaphoreType.DMA((2 + pieces,))],
    )(*arrays)


def per_device(
    ndp, nsec, section_inputs, norm_gain, down_proj, up_proj, readout_matrix, ground_truth_series, valid_len
):
    _, ntok, width = section_inputs.shape
    _, blk, latw = down_proj.shape
    horizon = readout_matrix.shape[1]
    nmb = valid_len.shape[0]
    rows = ntok // nmb
    vmem = pl.BlockSpec(memory_space=pltpu.VMEM)
    dma = pltpu.SemaphoreType.DMA
    grads, dg, ug = pl.pallas_call(
        functools.partial(kernel, ndp, nsec),
        name="relay",
        out_shape=(
            jax.ShapeDtypeStruct((nmb, rows, width), BF16),
            jax.ShapeDtypeStruct((blk, latw), BF16),
            jax.ShapeDtypeStruct((latw, blk), BF16),
        ),
        in_specs=[vmem] * 6 + [pl.BlockSpec(memory_space=pltpu.SMEM)],
        out_specs=(pl.BlockSpec(memory_space=pl.ANY), vmem, vmem),
        scratch_shapes=[
            pltpu.VMEM((ndp, latw, blk), BF16),
            pltpu.VMEM((ndp, blk, latw), BF16),
            pltpu.VMEM((ndp, blk, horizon), BF16),
            pltpu.VMEM((ndp, ntok, blk), BF16),
            pltpu.VMEM((ndp, ntok, blk), BF16),
            pltpu.VMEM((ndp, ntok, latw), BF16),
            pltpu.VMEM((ntok, latw), F32),
            pltpu.VMEM((ntok, latw), F32),
            pltpu.VMEM((ntok, 128), F32),
            pltpu.VMEM((nmb, rows, width), BF16),
            pltpu.VMEM((ndp, nmb, rows, latw), BF16),
            pltpu.VMEM((ndp, nmb, rows, blk), BF16),
            pltpu.VMEM((nmb, rows, width), BF16),
            pltpu.VMEM((ntok, horizon), F32),
            dma,
            dma((2, ndp)),
            dma,
            dma,
            dma,
            dma,
            dma,
            dma,
            dma,
            dma,
            dma,
            dma((ndp, nmb // GROUP)),
            dma((nmb, SPLIT)),
            dma((nmb, SPLIT)),
            dma,
            dma,
            pltpu.SemaphoreType.REGULAR,
        ],
        compiler_params=pltpu.CompilerParams(collective_id=0, has_side_effects=True),
    )(
        section_inputs[0],
        norm_gain,
        down_proj[0],
        up_proj[0],
        readout_matrix,
        ground_truth_series,
        valid_len,
    )
    grads, dg, ug = hand_over(grads.reshape(ntok, width), dg, ug)
    return grads[None], dg[None], ug[None]


def solution(mesh):
    placed = (
        P("section", "dp", None),
        P("section", None),
        P("section", "dp", None),
        P("section", None, "dp"),
        P("dp", None),
        P("dp", None),
        P("dp"),
    )
    return jax.shard_map(
        functools.partial(per_device, mesh.shape["dp"], mesh.shape["section"]),
        mesh=mesh,
        in_specs=placed,
        out_specs=(P("section", "dp", None), P("section", "dp", None), P("section", None, "dp")),
        check_vma=False,
    )
```

```python
import functools

import jax
import jax.numpy as jnp
from jax import lax
from jax.experimental import pallas as pl
from jax.experimental.pallas import tpu as pltpu
from jax.sharding import PartitionSpec as P

EPSILON = 1e-05
MESH = pl.DeviceIdType.MESH
F32 = jnp.float32
BF16 = jnp.bfloat16
LINE = 4
GROUP = 2
SIDE = 128
LAG = 2
TOP = 8
SPLIT = 4
COT_GROUPS = 1


def matmul(left, right):
    return jnp.dot(left, right, preferred_element_type=F32)


def matmul_nt(left, right):
    return lax.dot_general(left, right, (((1,), (1,)), ((), ())), preferred_element_type=F32)


def matmul_tn(left, right):
    return lax.dot_general(left, right, (((0,), (0,)), ((), ())), preferred_element_type=F32)


def copy_to(src, dst, send, recv, dev):
    return pltpu.make_async_remote_copy(
        src_ref=src, dst_ref=dst, send_sem=send, recv_sem=recv, device_id=dev, device_id_type=MESH
    )


def kernel(
    ndp,
    nsec,
    x_ref,
    gain_ref,
    down_ref,
    up_ref,
    ro_ref,
    gt_ref,
    vl_ref,
    out_ref,
    dg_ref,
    ug_ref,
    wd,
    wu,
    ro,
    normed,
    ncols,
    act,
    lat,
    dsil,
    inv,
    inc,
    lg,
    cot,
    outp,
    est,
    cot_next,
    w_send,
    w_recv,
    ro_send,
    ro_recv,
    n_send,
    n_recv,
    a_send,
    a_recv,
    c_send,
    c_recv,
    l_send,
    l_recv,
    r_send,
    r_recv,
    own_sem,
    out_sem,
    x_send,
    x_recv,
    clear,
):
    nmb, rows, width = inc.shape
    ntok = nmb * rows
    blk = wd.shape[1]
    latw = wd.shape[2]
    sec = lax.axis_index("section")
    me = lax.axis_index("dp")
    ncol = ndp // LINE
    mx = me // LINE
    my = me % LINE
    last = nsec - 1

    def at(xx, yy):
        return {"dp": (xx % ncol) * LINE + yy % LINE}

    def peer(j):
        return (me + j) % ndp

    barrier = pltpu.get_barrier_semaphore()

    def greet(j, c):
        pl.semaphore_signal(barrier, inc=1, device_id={"dp": peer(j)}, device_id_type=MESH)
        return c

    lax.fori_loop(1, ndp, greet, 0)

    @pl.when(sec > 0)
    def _():
        pl.semaphore_signal(barrier, inc=1, device_id={"section": sec - 1}, device_id_type=MESH)

    @pl.when(sec < last)
    def _():
        pl.semaphore_signal(barrier, inc=1, device_id={"section": sec + 1}, device_id_type=MESH)

    wd[me] = down_ref[...].T
    wu[me] = up_ref[...].T
    ro[me] = ro_ref[...]

    @pl.when((sec > 0) & (sec < last))
    def _():
        pl.semaphore_wait(barrier, ndp + 1)

    @pl.when((sec == 0) | (sec == last))
    def _():
        pl.semaphore_wait(barrier, ndp)

    pieces = (wd, wu)

    def send_block(e, k, dev):
        copy_to(pieces[k].at[e], pieces[k].at[e], w_send, w_recv.at[k, e], dev).start()

    def wait_block(e, k):
        copy_to(pieces[k].at[e], pieces[k].at[e], w_send, w_recv.at[k, e], at(mx, my)).wait_recv()

    left, right = at(mx + ncol - 1, my), at(mx + 1, my)
    order = (my, 1 + my % 2, (my * 3 + 2) % 5, 3 * (1 - my // 2))

    def column(shift, row):
        return ((mx + shift + ncol) % ncol) * LINE + row

    even = sec % 2 == 0
    odd = sec % 2 == 1


    for k in (0, 1):
        send_block(me, k, left)
        send_block(me, k, right)
        for row in order[1:]:
            send_block(me, k, at(mx, row))

    @pl.when(sec == last)
    def _():
        def send_ro(j, c):
            copy_to(ro.at[me], ro.at[me], ro_send, ro_recv, {"dp": peer(j)}).start()
            return c

        lax.fori_loop(1, ndp, send_ro, 0)

    gain = gain_ref[...].astype(F32)
    values = x_ref[...].astype(F32)
    inverse = lax.rsqrt(jnp.mean(values * values, axis=-1, keepdims=True) + EPSILON)
    inv[...] = jnp.broadcast_to(inverse, inv.shape)
    for b in range(ndp):
        cols = slice(b * blk, (b + 1) * blk)
        unit = x_ref[:, cols].astype(F32) * inverse
        normed[b] = (unit * gain[:, cols]).astype(BF16)

    for k, near, way in ((0, -1, right), (1, 1, left)):
        for i in range(1, LINE + 1):
            if i < LINE:
                e = column(0, order[i])
                wait_block(e, k)
                send_block(e, k, left)
                send_block(e, k, right)
            e = column(near, order[i - 1])
            wait_block(e, k)
            send_block(e, k, way)
    for row in order:
        wait_block(column(1, row), 0)
        wait_block(column(2, row), 0)

    def latent_step(b, acc):
        return acc + matmul_nt(normed[b], wd[b])

    latent = lax.fori_loop(0, ndp, latent_step, jnp.zeros((ntok, latw), F32))
    lat[...] = latent
    sigmoid = jax.nn.sigmoid(latent)
    activated = (latent * sigmoid).astype(BF16)
    act[me] = activated
    dsil[...] = sigmoid * (1.0 + latent * (1.0 - sigmoid))

    def forecast(e, first=False):
        cols = pl.ds(pl.multiple_of(e * blk, blk), blk)
        adapter = x_ref[:, cols].astype(F32) + matmul_nt(act[me], wu[e])
        part = matmul(adapter.astype(BF16), ro[e])
        est[...] = part if first else est[...] + part

    @pl.when(sec == last)
    def _():
        copy_to(ro.at[pl.ds(0, ndp - 1)], ro.at[pl.ds(0, ndp - 1)], ro_send, ro_recv, at(mx, my)).wait_recv()
        forecast(me, True)
        for row in order[1:]:
            forecast(column(0, row))
        for row in order:
            forecast(column(1, row))

    for shift in (-1, 2):
        for row in order:
            wait_block(column(shift, row), 1)

            @pl.when(sec == last)
            def _(shift=shift, row=row):
                forecast(column(shift, row))

    @pl.when(sec == last)
    def _():
        diff = est[...] - gt_ref[...]
        offset = lax.broadcasted_iota(jnp.int32, (rows, diff.shape[1]), 0)
        errs = []
        for m in range(nmb):
            mask = jnp.where(offset < vl_ref[m], 1.0, 0.0)
            errs.append(mask * diff[m * rows : (m + 1) * rows])
        error = jnp.concatenate(errs, axis=0).astype(BF16)
        for b in range(ndp):
            cols = slice(b * blk, (b + 1) * blk)
            top = matmul_nt(error, ro[b]).astype(BF16)
            inc[:, :, cols] = top.reshape(nmb, rows, blk)

    def send_early(j, c):
        p = peer(j)
        copy_to(act.at[me], act.at[me], a_send, a_recv, {"dp": p}).start()
        copy_to(normed.at[p], ncols.at[me], n_send, n_recv, {"dp": p}).start()
        return c

    @pl.when(even & (sec < nsec - TOP))
    def _():
        pl.semaphore_signal(clear, inc=1, device_id={"section": sec + 1}, device_id_type=MESH)

    @pl.when(jnp.logical_not(even) & (sec < nsec - TOP))
    def _():
        pl.semaphore_wait(clear, 1)

    @pl.when(sec < nsec - TOP)
    def _():
        lax.fori_loop(1, ndp, send_early, 0)

    ncols[me] = normed[me]

    below = {"section": (sec + last) % nsec}
    per = ndp // SPLIT

    def relay_copy(m, q):
        cols = slice(q * per * blk, (q + 1) * per * blk)
        return copy_to(outp.at[m, :, cols], inc.at[m, :, cols], r_send.at[m, q], r_recv.at[m, q], below)

    def step(m, c):
        tok = pl.ds(pl.multiple_of(m * rows, rows), rows)
        h = jnp.zeros((rows, latw), F32)
        for q in range(SPLIT):

            @pl.when(sec < last)
            def _(q=q):
                relay_copy(m, q).wait_recv()

            for b in range(q * per, (q + 1) * per):
                h = h + matmul(inc[m, :, b * blk : (b + 1) * blk], wu[b])
        latent_grad = (h * dsil[tok, :]).astype(BF16)
        lg[me, m, :, 0:latw] = latent_grad
        iv = inv[tok, 0:1]
        mean = jnp.sum(latent_grad.astype(F32) * lat[tok, :], axis=-1, keepdims=True) * (1.0 / width)
        lane = lax.broadcasted_iota(jnp.int32, (rows, SIDE), 1)
        lg[me, m, :, latw:] = jnp.where(lane < SIDE // 2, iv, iv * mean).astype(BF16)
        for q in range(SPLIT):
            for b in range(q * per, (q + 1) * per):
                cols = slice(b * blk, (b + 1) * blk)
                scaled = matmul(latent_grad, wd[b]) * gain_ref[:, cols].astype(F32)
                unit = x_ref[tok, cols].astype(F32) * iv
                g = inc[m, :, cols].astype(F32) + iv * (scaled - unit * mean)
                outp[m, :, cols] = g.astype(BF16)

            @pl.when(sec > 0)
            def _(q=q):
                relay_copy(m, q).start()

        return c

    own_cols = pl.ds(pl.multiple_of(me * blk, blk), blk)

    def send_lg(e, g, dev):
        part = pl.ds(g * GROUP, GROUP)
        copy_to(lg.at[e, part], lg.at[e, part], l_send, l_recv.at[e, g], dev).start()

    def wait_lg(e, g):
        part = pl.ds(g * GROUP, GROUP)
        copy_to(lg.at[e, part], lg.at[e, part], l_send, l_recv.at[e, g], left).wait_recv()

    def pass_on(g):
        @pl.when(g < groups)
        def _():
            send_lg(me, g, left)
            send_lg(me, g, right)
            for row in order[1:]:
                send_lg(me, g, at(mx, row))
        def send_columns():
            part = pl.ds((g + 1 - COT_GROUPS) * GROUP, GROUP * COT_GROUPS)

            def send_cot(j, c):
                p = peer(j)
                p_cols = pl.ds(pl.multiple_of(p * blk, blk), blk)
                copy_to(inc.at[part, :, p_cols], cot.at[me, part], c_send, c_recv, {"dp": p}).start()
                return c

            lax.fori_loop(1, ndp, send_cot, 0)

        @pl.when((g < groups) & (g % COT_GROUPS == COT_GROUPS - 1))
        def _():
            pl.when(odd)(send_columns)

        @pl.when((g >= LAG) & (g < groups + LAG))
        def _():
            for row in order[1:]:
                wait_lg(column(0, row), g - LAG)
                send_lg(column(0, row), g - LAG, left)
                send_lg(column(0, row), g - LAG, right)

        @pl.when(g >= 2 * LAG)
        def _():
            for n, row in enumerate(order):
                near = 1 if n % 2 else -1
                e = column(near, row)
                wait_lg(e, g - 2 * LAG)
                send_lg(e, g - 2 * LAG, left if n % 2 else right)

    groups = nmb // GROUP

    def stretch(g, c):
        lax.fori_loop(g * GROUP, (g + 1) * GROUP, step, 0)
        part = pl.ds(g * GROUP, GROUP)
        pltpu.make_async_copy(outp.at[part], out_ref.at[part], out_sem).start()
        pass_on(g)
        return c

    lax.fori_loop(0, groups, stretch, 0)
    for g in range(groups, groups + 2 * LAG):
        pass_on(g)

    @pl.when(sec >= nsec - TOP)
    def _():
        lax.fori_loop(1, ndp, send_early, 0)

    own = pltpu.make_async_copy(inc.at[:, :, own_cols], cot.at[me], own_sem)

    @pl.when(odd)
    def _():
        own.start()
        own.wait()

    others = pl.ds(0, ndp - 1)
    def last_lg(g, c):
        for n, row in enumerate(order):
            wait_lg(column(-1 if n % 2 else 1, row), g)
            wait_lg(column(2, row), g)
        return c

    lax.fori_loop(0, groups, last_lg, 0)
    copy_to(ncols.at[others], ncols.at[others], n_send, n_recv, at(mx, my)).wait_recv()

    def ship(e):
        return copy_to(cot_next.at[e], cot.at[e], x_send, x_recv, below)

    @pl.when(odd)
    def _():
        copy_to(cot.at[others], cot.at[others], c_send, c_recv, at(mx, my)).wait_recv()
        gain_own = gain_ref[:, own_cols].astype(F32)
        gain_inv = 1.0 / gain_own

        def next_cols(e, c):
            side = lg[e, :, :, latw:].reshape(ntok, SIDE).astype(F32)
            scaled = matmul(lg[e, :, :, 0:latw].reshape(ntok, latw), wd[me]) * gain_own
            unit = ncols[e].astype(F32) * gain_inv
            grad = cot[e].reshape(ntok, blk).astype(F32) + side[:, 0:1] * scaled - side[:, SIDE // 2 : SIDE // 2 + 1] * unit
            cot_next[e] = grad.astype(BF16).reshape(nmb, rows, blk)
            ship(e).start()
            return c

        lax.fori_loop(0, ndp, next_cols, 0)

    dg = matmul_tn(ncols[...].reshape(ndp * ntok, blk), lg[:, :, :, 0:latw].reshape(ndp * ntok, latw))
    dg_ref[...] = dg.astype(BF16)
    copy_to(act.at[others], act.at[others], a_send, a_recv, at(mx, my)).wait_recv()

    @pl.when(even)
    def _():
        copy_to(cot, cot, x_send, x_recv, below).wait_recv()

    ug = matmul_tn(act[...].reshape(ndp * ntok, latw), cot[...].reshape(ndp * ntok, blk))
    ug_ref[...] = ug.astype(BF16)

    pltpu.make_async_copy(outp, out_ref, out_sem).wait()
    for k in (0, 1):
        copy_to(pieces[k].at[others], pieces[k].at[others], w_send, w_recv.at[k, 0], at(mx, my)).wait_send()

    @pl.when(sec == last)
    def _():
        copy_to(ro.at[others], ro.at[others], ro_send, ro_recv, at(mx, my)).wait_send()

    copy_to(act.at[others], act.at[others], a_send, a_recv, at(mx, my)).wait_send()
    copy_to(ncols.at[others], ncols.at[others], n_send, n_recv, at(mx, my)).wait_send()

    @pl.when(odd)
    def _():
        copy_to(cot.at[others], cot.at[others], c_send, c_recv, at(mx, my)).wait_send()
        copy_to(cot_next, cot, x_send, x_recv, below).wait_send()

    copy_to(lg.at[others], lg.at[others], l_send, l_recv.at[0, 0], left).wait_send()

    @pl.when(sec > 0)
    def _():
        def gone(m, c):
            for q in range(SPLIT):
                relay_copy(m, q).wait_send()
            return c

        lax.fori_loop(0, nmb, gone, 0)


def hand_over_kernel(pieces, a_in, b_in, c_in, a_out, b_out, c_out, a_buf, b_buf, c_buf, in_sem, out_sem):
    rows = a_buf.shape[0] // pieces
    jobs = [(b_in, b_buf, b_out), (c_in, c_buf, c_out)]
    for i in range(pieces):
        part = pl.ds(i * rows, rows)
        jobs.append((a_in.at[part], a_buf.at[part], a_out.at[part]))
    for i, (src, buf, _) in enumerate(jobs):
        pltpu.make_async_copy(src, buf, in_sem.at[i]).start()
    for i, (src, buf, dst) in enumerate(jobs):
        pltpu.make_async_copy(src, buf, in_sem.at[i]).wait()
        pltpu.make_async_copy(buf, dst, out_sem.at[i]).start()
    for i, (_, buf, dst) in enumerate(jobs):
        pltpu.make_async_copy(buf, dst, out_sem.at[i]).wait()


def hand_over(*arrays, pieces=4):
    anywhere = pl.BlockSpec(memory_space=pl.ANY)
    return pl.pallas_call(
        functools.partial(hand_over_kernel, pieces),
        name="hand_over",
        out_shape=tuple(jax.ShapeDtypeStruct(a.shape, a.dtype) for a in arrays),
        in_specs=[anywhere] * 3,
        out_specs=(anywhere,) * 3,
        scratch_shapes=[pltpu.VMEM(a.shape, a.dtype) for a in arrays]
        + [pltpu.SemaphoreType.DMA((2 + pieces,)), pltpu.SemaphoreType.DMA((2 + pieces,))],
    )(*arrays)


def per_device(
    ndp, nsec, section_inputs, norm_gain, down_proj, up_proj, readout_matrix, ground_truth_series, valid_len
):
    _, ntok, width = section_inputs.shape
    _, blk, latw = down_proj.shape
    horizon = readout_matrix.shape[1]
    nmb = valid_len.shape[0]
    rows = ntok // nmb
    vmem = pl.BlockSpec(memory_space=pltpu.VMEM)
    dma = pltpu.SemaphoreType.DMA
    grads, dg, ug = pl.pallas_call(
        functools.partial(kernel, ndp, nsec),
        name="relay",
        out_shape=(
            jax.ShapeDtypeStruct((nmb, rows, width), BF16),
            jax.ShapeDtypeStruct((blk, latw), BF16),
            jax.ShapeDtypeStruct((latw, blk), BF16),
        ),
        in_specs=[vmem] * 6 + [pl.BlockSpec(memory_space=pltpu.SMEM)],
        out_specs=(pl.BlockSpec(memory_space=pl.ANY), vmem, vmem),
        scratch_shapes=[
            pltpu.VMEM((ndp, latw, blk), BF16),
            pltpu.VMEM((ndp, blk, latw), BF16),
            pltpu.VMEM((ndp, blk, horizon), BF16),
            pltpu.VMEM((ndp, ntok, blk), BF16),
            pltpu.VMEM((ndp, ntok, blk), BF16),
            pltpu.VMEM((ndp, ntok, latw), BF16),
            pltpu.VMEM((ntok, latw), F32),
            pltpu.VMEM((ntok, latw), F32),
            pltpu.VMEM((ntok, 128), F32),
            pltpu.VMEM((nmb, rows, width), BF16),
            pltpu.VMEM((ndp, nmb, rows, latw + SIDE), BF16),
            pltpu.VMEM((ndp, nmb, rows, blk), BF16),
            pltpu.VMEM((nmb, rows, width), BF16),
            pltpu.VMEM((ntok, horizon), F32),
            pltpu.VMEM((ndp, nmb, rows, blk), BF16),
            dma,
            dma((2, ndp)),
            dma,
            dma,
            dma,
            dma,
            dma,
            dma,
            dma,
            dma,
            dma,
            dma((ndp, nmb // GROUP)),
            dma((nmb, SPLIT)),
            dma((nmb, SPLIT)),
            dma,
            dma,
            dma,
            dma,
            pltpu.SemaphoreType.REGULAR,
        ],
        compiler_params=pltpu.CompilerParams(collective_id=0, has_side_effects=True),
    )(
        section_inputs[0],
        norm_gain,
        down_proj[0],
        up_proj[0],
        readout_matrix,
        ground_truth_series,
        valid_len,
    )
    grads, dg, ug = hand_over(grads.reshape(ntok, width), dg, ug)
    return grads[None], dg[None], ug[None]


def solution(mesh):
    placed = (
        P("section", "dp", None),
        P("section", None),
        P("section", "dp", None),
        P("section", None, "dp"),
        P("dp", None),
        P("dp", None),
        P("dp"),
    )
    return jax.shard_map(
        functools.partial(per_device, mesh.shape["dp"], mesh.shape["section"]),
        mesh=mesh,
        in_specs=placed,
        out_specs=(P("section", "dp", None), P("section", "dp", None), P("section", None, "dp")),
        check_vma=False,
    )
```

```python
import functools

import jax
import jax.numpy as jnp
from jax import lax
from jax.experimental import pallas as pl
from jax.experimental.pallas import tpu as pltpu
from jax.sharding import PartitionSpec as P

EPSILON = 1e-05
MESH = pl.DeviceIdType.MESH
F32 = jnp.float32
BF16 = jnp.bfloat16
LINE = 4
ROWS = 8
GROUP = 4
SIDE = 128
LAG = 2
TOP = 8
SPLIT = 2
COT_GROUPS = 1


def matmul(left, right):
    return jnp.dot(left, right, preferred_element_type=F32)


def matmul_nt(left, right):
    return lax.dot_general(left, right, (((1,), (1,)), ((), ())), preferred_element_type=F32)


def matmul_tn(left, right):
    return lax.dot_general(left, right, (((0,), (0,)), ((), ())), preferred_element_type=F32)


def flat(values, rows):
    return values.astype(F32).reshape(rows, values.shape[-1]).astype(BF16)


def copy_to(src, dst, send, recv, dev):
    return pltpu.make_async_remote_copy(
        src_ref=src, dst_ref=dst, send_sem=send, recv_sem=recv, device_id=dev, device_id_type=MESH
    )


def kernel(
    ndp,
    nsec,
    x_ref,
    gain_ref,
    down_ref,
    up_ref,
    ro_ref,
    gt_ref,
    vl_ref,
    out_ref,
    dg_ref,
    ug_ref,
    wd,
    wu,
    ro,
    normed,
    ncols,
    act,
    lat,
    dsil,
    inv,
    inc,
    lg,
    cot,
    outp,
    est,
    cot_next,
    w_send,
    w_recv,
    ro_send,
    ro_recv,
    n_send,
    n_recv,
    a_send,
    a_recv,
    c_send,
    c_recv,
    l_send,
    l_recv,
    r_send,
    r_recv,
    own_sem,
    out_sem,
    x_send,
    x_recv,
    clear,
):
    nmb, rows, width = inc.shape
    ntok = nmb * rows
    blk = wd.shape[1]
    latw = wd.shape[2]
    sec = lax.axis_index("section")
    me = lax.axis_index("dp")
    ncol = ndp // LINE
    mx = me // LINE
    my = me % LINE
    last = nsec - 1

    def at(xx, yy):
        return {"dp": (xx % ncol) * LINE + yy % LINE}

    def peer(j):
        return (me + j) % ndp

    barrier = pltpu.get_barrier_semaphore()

    def greet(j, c):
        pl.semaphore_signal(barrier, inc=1, device_id={"dp": peer(j)}, device_id_type=MESH)
        return c

    lax.fori_loop(1, ndp, greet, 0)

    @pl.when(sec > 0)
    def _():
        pl.semaphore_signal(barrier, inc=1, device_id={"section": sec - 1}, device_id_type=MESH)

    @pl.when(sec < last)
    def _():
        pl.semaphore_signal(barrier, inc=1, device_id={"section": sec + 1}, device_id_type=MESH)

    wd[me] = down_ref[...].T
    wu[me] = up_ref[...].T
    ro[me] = ro_ref[...]

    @pl.when((sec > 0) & (sec < last))
    def _():
        pl.semaphore_wait(barrier, ndp + 1)

    @pl.when((sec == 0) | (sec == last))
    def _():
        pl.semaphore_wait(barrier, ndp)

    pieces = (wd, wu)

    def send_block(e, k, dev):
        copy_to(pieces[k].at[e], pieces[k].at[e], w_send, w_recv.at[k, e], dev).start()

    def wait_block(e, k):
        copy_to(pieces[k].at[e], pieces[k].at[e], w_send, w_recv.at[k, e], at(mx, my)).wait_recv()

    left, right = at(mx + ncol - 1, my), at(mx + 1, my)
    order = (my, 1 + my % 2, (my * 3 + 2) % 5, 3 * (1 - my // 2))

    def column(shift, row):
        return ((mx + shift + ncol) % ncol) * LINE + row

    even = sec % 2 == 0
    odd = sec % 2 == 1


    for k in (0, 1):
        send_block(me, k, left)
        send_block(me, k, right)
        for row in order[1:]:
            send_block(me, k, at(mx, row))

    @pl.when(sec == last)
    def _():
        def send_ro(j, c):
            copy_to(ro.at[me], ro.at[me], ro_send, ro_recv, {"dp": peer(j)}).start()
            return c

        lax.fori_loop(1, ndp, send_ro, 0)

    gain = gain_ref[...].astype(F32)
    values = x_ref[...].astype(F32).reshape(ntok, width)
    inverse = lax.rsqrt(jnp.mean(values * values, axis=-1, keepdims=True) + EPSILON)
    inv[...] = jnp.broadcast_to(inverse, inv.shape)
    for b in range(ndp):
        cols = slice(b * blk, (b + 1) * blk)
        unit = x_ref[:, :, cols].astype(F32).reshape(ntok, blk) * inverse
        normed[b] = (unit * gain[:, cols]).astype(BF16)

    for k, near, way in ((0, -1, right), (1, 1, left)):
        for i in range(1, LINE + 1):
            if i < LINE:
                e = column(0, order[i])
                wait_block(e, k)
                send_block(e, k, left)
                send_block(e, k, right)
            e = column(near, order[i - 1])
            wait_block(e, k)
            send_block(e, k, way)
    for row in order:
        wait_block(column(1, row), 0)
        wait_block(column(2, row), 0)

    def latent_step(b, acc):
        return acc + matmul_nt(normed[b], wd[b])

    latent = lax.fori_loop(0, ndp, latent_step, jnp.zeros((ntok, latw), F32))
    lat[...] = latent
    sigmoid = jax.nn.sigmoid(latent)
    activated = (latent * sigmoid).astype(BF16)
    act[me] = activated
    dsil[...] = sigmoid * (1.0 + latent * (1.0 - sigmoid))

    def forecast(e, first=False):
        cols = pl.ds(pl.multiple_of(e * blk, blk), blk)
        adapter = x_ref[:, :, cols].astype(F32).reshape(ntok, blk) + matmul_nt(act[me], wu[e])
        part = matmul(adapter.astype(BF16), ro[e])
        est[...] = part if first else est[...] + part

    @pl.when(sec == last)
    def _():
        copy_to(ro.at[pl.ds(0, ndp - 1)], ro.at[pl.ds(0, ndp - 1)], ro_send, ro_recv, at(mx, my)).wait_recv()
        forecast(me, True)
        for row in order[1:]:
            forecast(column(0, row))
        for row in order:
            forecast(column(1, row))

    for shift in (-1, 2):
        for row in order:
            wait_block(column(shift, row), 1)

            @pl.when(sec == last)
            def _(shift=shift, row=row):
                forecast(column(shift, row))

    @pl.when(sec == last)
    def _():
        diff = est[...] - gt_ref[...]
        micro = ntok // vl_ref.shape[0]
        offset = lax.broadcasted_iota(jnp.int32, (micro, diff.shape[1]), 0)
        errs = []
        for m in range(vl_ref.shape[0]):
            mask = jnp.where(offset < vl_ref[m], 1.0, 0.0)
            errs.append(mask * diff[m * micro : (m + 1) * micro])
        error = jnp.concatenate(errs, axis=0).astype(BF16)
        for b in range(ndp):
            cols = slice(b * blk, (b + 1) * blk)
            top = matmul_nt(error, ro[b])
            inc[:, :, cols] = top.reshape(nmb, rows, blk).astype(BF16)

    def send_early(j, c):
        p = peer(j)
        copy_to(act.at[me], act.at[me], a_send, a_recv, {"dp": p}).start()
        copy_to(normed.at[p], ncols.at[me], n_send, n_recv, {"dp": p}).start()
        return c

    @pl.when(even & (sec < nsec - TOP))
    def _():
        pl.semaphore_signal(clear, inc=1, device_id={"section": sec + 1}, device_id_type=MESH)

    @pl.when(jnp.logical_not(even) & (sec < nsec - TOP))
    def _():
        pl.semaphore_wait(clear, 1)

    @pl.when(sec < nsec - TOP)
    def _():
        lax.fori_loop(1, ndp, send_early, 0)

    ncols[me] = normed[me]

    below = {"section": (sec + last) % nsec}
    per = ndp // SPLIT

    def relay_copy(m, q):
        cols = slice(q * per * blk, (q + 1) * per * blk)
        return copy_to(outp.at[m, :, cols], inc.at[m, :, cols], r_send.at[m, q], r_recv.at[m, q], below)

    def step(m, c):
        tok = pl.ds(pl.multiple_of(m * rows, rows), rows)
        h = jnp.zeros((rows, latw), F32)
        for q in range(SPLIT):

            @pl.when(sec < last)
            def _(q=q):
                relay_copy(m, q).wait_recv()

            for b in range(q * per, (q + 1) * per):
                h = h + matmul(inc[m, :, b * blk : (b + 1) * blk], wu[b])
        latent_grad = (h * dsil[tok, :]).astype(BF16)
        lg[me, m, :, 0:latw] = latent_grad
        iv = inv[tok, 0:1]
        mean = jnp.sum(latent_grad.astype(F32) * lat[tok, :], axis=-1, keepdims=True) * (1.0 / width)
        lane = lax.broadcasted_iota(jnp.int32, (rows, SIDE), 1)
        lg[me, m, :, latw:] = jnp.where(lane < SIDE // 2, iv, iv * mean).astype(BF16)
        for q in range(SPLIT):
            for b in range(q * per, (q + 1) * per):
                cols = slice(b * blk, (b + 1) * blk)
                scaled = matmul(latent_grad, wd[b]) * gain_ref[:, cols].astype(F32)
                unit = x_ref[m, :, cols].astype(F32) * iv
                g = inc[m, :, cols].astype(F32) + iv * (scaled - unit * mean)
                outp[m, :, cols] = g.astype(BF16)

            @pl.when(sec > 0)
            def _(q=q):
                relay_copy(m, q).start()

        return c

    own_cols = pl.ds(pl.multiple_of(me * blk, blk), blk)

    def send_lg(e, g, dev):
        part = pl.ds(g * GROUP, GROUP)
        copy_to(lg.at[e, part], lg.at[e, part], l_send, l_recv.at[e, g], dev).start()

    def wait_lg(e, g):
        part = pl.ds(g * GROUP, GROUP)
        copy_to(lg.at[e, part], lg.at[e, part], l_send, l_recv.at[e, g], left).wait_recv()

    def pass_on(g):
        @pl.when(g < groups)
        def _():
            send_lg(me, g, left)
            send_lg(me, g, right)
            for row in order[1:]:
                send_lg(me, g, at(mx, row))
        def send_columns():
            part = pl.ds((g + 1 - COT_GROUPS) * GROUP, GROUP * COT_GROUPS)

            def send_cot(j, c):
                p = peer(j)
                p_cols = pl.ds(pl.multiple_of(p * blk, blk), blk)
                copy_to(inc.at[part, :, p_cols], cot.at[me, part], c_send, c_recv, {"dp": p}).start()
                return c

            lax.fori_loop(1, ndp, send_cot, 0)

        @pl.when((g < groups) & (g % COT_GROUPS == COT_GROUPS - 1))
        def _():
            pl.when(odd)(send_columns)

        @pl.when((g >= LAG) & (g < groups + LAG))
        def _():
            for row in order[1:]:
                wait_lg(column(0, row), g - LAG)
                send_lg(column(0, row), g - LAG, left)
                send_lg(column(0, row), g - LAG, right)

        @pl.when(g >= 2 * LAG)
        def _():
            for n, row in enumerate(order):
                near = 1 if n % 2 else -1
                e = column(near, row)
                wait_lg(e, g - 2 * LAG)
                send_lg(e, g - 2 * LAG, left if n % 2 else right)

    groups = nmb // GROUP

    def stretch(g, c):
        lax.fori_loop(g * GROUP, (g + 1) * GROUP, step, 0)
        part = pl.ds(g * GROUP, GROUP)
        pltpu.make_async_copy(outp.at[part], out_ref.at[part], out_sem).start()
        pass_on(g)
        return c

    lax.fori_loop(0, groups, stretch, 0)
    for g in range(groups, groups + 2 * LAG):
        pass_on(g)

    @pl.when(sec >= nsec - TOP)
    def _():
        lax.fori_loop(1, ndp, send_early, 0)

    own = pltpu.make_async_copy(inc.at[:, :, own_cols], cot.at[me], own_sem)

    @pl.when(odd)
    def _():
        own.start()
        own.wait()

    others = pl.ds(0, ndp - 1)
    def last_lg(g, c):
        for n, row in enumerate(order):
            wait_lg(column(-1 if n % 2 else 1, row), g)
            wait_lg(column(2, row), g)
        return c

    lax.fori_loop(0, groups, last_lg, 0)
    copy_to(ncols.at[others], ncols.at[others], n_send, n_recv, at(mx, my)).wait_recv()

    def ship(e):
        return copy_to(cot_next.at[e], cot.at[e], x_send, x_recv, below)

    @pl.when(odd)
    def _():
        copy_to(cot.at[others], cot.at[others], c_send, c_recv, at(mx, my)).wait_recv()
        gain_own = gain_ref[:, own_cols].astype(F32)
        gain_inv = 1.0 / gain_own

        def next_cols(e, c):
            side = lg[e, :, :, latw:].astype(F32).reshape(ntok, SIDE)
            scaled = matmul(flat(lg[e, :, :, 0:latw], ntok), wd[me]) * gain_own
            unit = ncols[e].astype(F32) * gain_inv
            grad = cot[e].astype(F32).reshape(ntok, blk) + side[:, 0:1] * scaled - side[:, SIDE // 2 : SIDE // 2 + 1] * unit
            cot_next[e] = grad.reshape(nmb, rows, blk).astype(BF16)
            ship(e).start()
            return c

        lax.fori_loop(0, ndp, next_cols, 0)

    dg = matmul_tn(ncols[...].reshape(ndp * ntok, blk), flat(lg[:, :, :, 0:latw], ndp * ntok))
    dg_ref[...] = dg.astype(BF16)
    copy_to(act.at[others], act.at[others], a_send, a_recv, at(mx, my)).wait_recv()

    @pl.when(even)
    def _():
        copy_to(cot, cot, x_send, x_recv, below).wait_recv()

    ug = matmul_tn(act[...].reshape(ndp * ntok, latw), flat(cot[...], ndp * ntok))
    ug_ref[...] = ug.astype(BF16)

    pltpu.make_async_copy(outp, out_ref, out_sem).wait()
    for k in (0, 1):
        copy_to(pieces[k].at[others], pieces[k].at[others], w_send, w_recv.at[k, 0], at(mx, my)).wait_send()

    @pl.when(sec == last)
    def _():
        copy_to(ro.at[others], ro.at[others], ro_send, ro_recv, at(mx, my)).wait_send()

    copy_to(act.at[others], act.at[others], a_send, a_recv, at(mx, my)).wait_send()
    copy_to(ncols.at[others], ncols.at[others], n_send, n_recv, at(mx, my)).wait_send()

    @pl.when(odd)
    def _():
        copy_to(cot.at[others], cot.at[others], c_send, c_recv, at(mx, my)).wait_send()
        copy_to(cot_next, cot, x_send, x_recv, below).wait_send()

    copy_to(lg.at[others], lg.at[others], l_send, l_recv.at[0, 0], left).wait_send()

    @pl.when(sec > 0)
    def _():
        def gone(m, c):
            for q in range(SPLIT):
                relay_copy(m, q).wait_send()
            return c

        lax.fori_loop(0, nmb, gone, 0)


def hand_over_kernel(pieces, a_in, b_in, c_in, a_out, b_out, c_out, a_buf, b_buf, c_buf, in_sem, out_sem):
    rows = a_buf.shape[0] // pieces
    jobs = [(b_in, b_buf, b_out), (c_in, c_buf, c_out)]
    for i in range(pieces):
        part = pl.ds(i * rows, rows)
        jobs.append((a_in.at[part], a_buf.at[part], a_out.at[part]))
    for i, (src, buf, _) in enumerate(jobs):
        pltpu.make_async_copy(src, buf, in_sem.at[i]).start()
    for i, (src, buf, dst) in enumerate(jobs):
        pltpu.make_async_copy(src, buf, in_sem.at[i]).wait()
        pltpu.make_async_copy(buf, dst, out_sem.at[i]).start()
    for i, (_, buf, dst) in enumerate(jobs):
        pltpu.make_async_copy(buf, dst, out_sem.at[i]).wait()


def hand_over(*arrays, pieces=4):
    anywhere = pl.BlockSpec(memory_space=pl.ANY)
    return pl.pallas_call(
        functools.partial(hand_over_kernel, pieces),
        name="hand_over",
        out_shape=tuple(jax.ShapeDtypeStruct(a.shape, a.dtype) for a in arrays),
        in_specs=[anywhere] * 3,
        out_specs=(anywhere,) * 3,
        scratch_shapes=[pltpu.VMEM(a.shape, a.dtype) for a in arrays]
        + [pltpu.SemaphoreType.DMA((2 + pieces,)), pltpu.SemaphoreType.DMA((2 + pieces,))],
    )(*arrays)


def per_device(
    ndp, nsec, section_inputs, norm_gain, down_proj, up_proj, readout_matrix, ground_truth_series, valid_len
):
    _, ntok, width = section_inputs.shape
    _, blk, latw = down_proj.shape
    horizon = readout_matrix.shape[1]
    rows = ROWS
    nmb = ntok // rows
    vmem = pl.BlockSpec(memory_space=pltpu.VMEM)
    dma = pltpu.SemaphoreType.DMA
    grads, dg, ug = pl.pallas_call(
        functools.partial(kernel, ndp, nsec),
        name="relay",
        out_shape=(
            jax.ShapeDtypeStruct((nmb, rows, width), BF16),
            jax.ShapeDtypeStruct((blk, latw), BF16),
            jax.ShapeDtypeStruct((latw, blk), BF16),
        ),
        in_specs=[vmem] * 6 + [pl.BlockSpec(memory_space=pltpu.SMEM)],
        out_specs=(pl.BlockSpec(memory_space=pl.ANY), vmem, vmem),
        scratch_shapes=[
            pltpu.VMEM((ndp, latw, blk), BF16),
            pltpu.VMEM((ndp, blk, latw), BF16),
            pltpu.VMEM((ndp, blk, horizon), BF16),
            pltpu.VMEM((ndp, ntok, blk), BF16),
            pltpu.VMEM((ndp, ntok, blk), BF16),
            pltpu.VMEM((ndp, ntok, latw), BF16),
            pltpu.VMEM((ntok, latw), F32),
            pltpu.VMEM((ntok, latw), F32),
            pltpu.VMEM((ntok, 128), F32),
            pltpu.VMEM((nmb, rows, width), BF16),
            pltpu.VMEM((ndp, nmb, rows, latw + SIDE), BF16),
            pltpu.VMEM((ndp, nmb, rows, blk), BF16),
            pltpu.VMEM((nmb, rows, width), BF16),
            pltpu.VMEM((ntok, horizon), F32),
            pltpu.VMEM((ndp, nmb, rows, blk), BF16),
            dma,
            dma((2, ndp)),
            dma,
            dma,
            dma,
            dma,
            dma,
            dma,
            dma,
            dma,
            dma,
            dma((ndp, nmb // GROUP)),
            dma((nmb, SPLIT)),
            dma((nmb, SPLIT)),
            dma,
            dma,
            dma,
            dma,
            pltpu.SemaphoreType.REGULAR,
        ],
        compiler_params=pltpu.CompilerParams(collective_id=0, has_side_effects=True),
    )(
        section_inputs.reshape(nmb, rows, width),
        norm_gain,
        down_proj[0],
        up_proj[0],
        readout_matrix,
        ground_truth_series,
        valid_len,
    )
    grads, dg, ug = hand_over(grads.reshape(ntok, width), dg, ug)
    return grads[None], dg[None], ug[None]


def solution(mesh):
    placed = (
        P("section", "dp", None),
        P("section", None),
        P("section", "dp", None),
        P("section", None, "dp"),
        P("dp", None),
        P("dp", None),
        P("dp"),
    )
    return jax.shard_map(
        functools.partial(per_device, mesh.shape["dp"], mesh.shape["section"]),
        mesh=mesh,
        in_specs=placed,
        out_specs=(P("section", "dp", None), P("section", "dp", None), P("section", None, "dp")),
        check_vma=False,
    )
```

```python
import functools

import jax
import jax.numpy as jnp
from jax import lax
from jax.experimental import pallas as pl
from jax.experimental.pallas import tpu as pltpu
from jax.sharding import PartitionSpec as P

EPSILON = 1e-05
MESH = pl.DeviceIdType.MESH
F32 = jnp.float32
BF16 = jnp.bfloat16
LINE = 4
ROWS = 8
GROUP = 2
SIDE = 128
LAG = 3
TOP = 8
SPLIT = 2
COT_GROUPS = 1


def matmul(left, right):
    return jnp.dot(left, right, preferred_element_type=F32)


def matmul_nt(left, right):
    return lax.dot_general(left, right, (((1,), (1,)), ((), ())), preferred_element_type=F32)


def matmul_tn(left, right):
    return lax.dot_general(left, right, (((0,), (0,)), ((), ())), preferred_element_type=F32)


def flat(values, rows):
    return values.astype(F32).reshape(rows, values.shape[-1]).astype(BF16)


def copy_to(src, dst, send, recv, dev):
    return pltpu.make_async_remote_copy(
        src_ref=src, dst_ref=dst, send_sem=send, recv_sem=recv, device_id=dev, device_id_type=MESH
    )


def kernel(
    ndp,
    nsec,
    x_ref,
    gain_ref,
    down_ref,
    up_ref,
    ro_ref,
    gt_ref,
    vl_ref,
    out_ref,
    dg_ref,
    ug_ref,
    wd,
    wu,
    ro,
    normed,
    ncols,
    act,
    lat,
    dsil,
    inv,
    inc,
    lg,
    cot,
    outp,
    est,
    cot_next,
    w_send,
    w_recv,
    ro_send,
    ro_recv,
    n_send,
    n_recv,
    a_send,
    a_recv,
    c_send,
    c_recv,
    l_send,
    l_recv,
    r_send,
    r_recv,
    own_sem,
    out_sem,
    x_send,
    x_recv,
    clear,
):
    nmb, rows, width = inc.shape
    ntok = nmb * rows
    blk = wd.shape[1]
    latw = wd.shape[2]
    sec = lax.axis_index("section")
    me = lax.axis_index("dp")
    ncol = ndp // LINE
    mx = me // LINE
    my = me % LINE
    last = nsec - 1

    def at(xx, yy):
        return {"dp": (xx % ncol) * LINE + yy % LINE}

    def peer(j):
        return (me + j) % ndp

    barrier = pltpu.get_barrier_semaphore()

    def greet(j, c):
        pl.semaphore_signal(barrier, inc=1, device_id={"dp": peer(j)}, device_id_type=MESH)
        return c

    lax.fori_loop(1, ndp, greet, 0)

    @pl.when(sec > 0)
    def _():
        pl.semaphore_signal(barrier, inc=1, device_id={"section": sec - 1}, device_id_type=MESH)

    @pl.when(sec < last)
    def _():
        pl.semaphore_signal(barrier, inc=1, device_id={"section": sec + 1}, device_id_type=MESH)

    wd[me] = down_ref[...].T
    wu[me] = up_ref[...].T
    ro[me] = ro_ref[...]

    @pl.when((sec > 0) & (sec < last))
    def _():
        pl.semaphore_wait(barrier, ndp + 1)

    @pl.when((sec == 0) | (sec == last))
    def _():
        pl.semaphore_wait(barrier, ndp)

    pieces = (wd, wu)

    def send_block(e, k, dev):
        copy_to(pieces[k].at[e], pieces[k].at[e], w_send, w_recv.at[k, e], dev).start()

    def wait_block(e, k):
        copy_to(pieces[k].at[e], pieces[k].at[e], w_send, w_recv.at[k, e], at(mx, my)).wait_recv()

    left, right = at(mx + ncol - 1, my), at(mx + 1, my)
    order = (my, 1 + my % 2, (my * 3 + 2) % 5, 3 * (1 - my // 2))

    def column(shift, row):
        return ((mx + shift + ncol) % ncol) * LINE + row

    even = sec % 2 == 0
    odd = sec % 2 == 1


    for k in (0, 1):
        send_block(me, k, left)
        send_block(me, k, right)
        for row in order[1:]:
            send_block(me, k, at(mx, row))

    @pl.when(sec == last)
    def _():
        def send_ro(j, c):
            copy_to(ro.at[me], ro.at[me], ro_send, ro_recv, {"dp": peer(j)}).start()
            return c

        lax.fori_loop(1, ndp, send_ro, 0)

    gain = gain_ref[...].astype(F32)
    values = x_ref[...].astype(F32).reshape(ntok, width)
    inverse = lax.rsqrt(jnp.mean(values * values, axis=-1, keepdims=True) + EPSILON)
    inv[...] = jnp.broadcast_to(inverse, inv.shape)
    for b in range(ndp):
        cols = slice(b * blk, (b + 1) * blk)
        unit = x_ref[:, :, cols].astype(F32).reshape(ntok, blk) * inverse
        normed[b] = (unit * gain[:, cols]).astype(BF16)

    for k, near, way in ((0, -1, right), (1, 1, left)):
        for i in range(1, LINE + 1):
            if i < LINE:
                e = column(0, order[i])
                wait_block(e, k)
                send_block(e, k, left)
                send_block(e, k, right)
            e = column(near, order[i - 1])
            wait_block(e, k)
            send_block(e, k, way)
    for row in order:
        wait_block(column(1, row), 0)
        wait_block(column(2, row), 0)

    def latent_step(b, acc):
        return acc + matmul_nt(normed[b], wd[b])

    latent = lax.fori_loop(0, ndp, latent_step, jnp.zeros((ntok, latw), F32))
    lat[...] = latent
    sigmoid = jax.nn.sigmoid(latent)
    activated = (latent * sigmoid).astype(BF16)
    act[me] = activated
    dsil[...] = sigmoid * (1.0 + latent * (1.0 - sigmoid))

    def forecast(e, first=False):
        cols = pl.ds(pl.multiple_of(e * blk, blk), blk)
        adapter = x_ref[:, :, cols].astype(F32).reshape(ntok, blk) + matmul_nt(act[me], wu[e])
        part = matmul(adapter.astype(BF16), ro[e])
        est[...] = part if first else est[...] + part

    @pl.when(sec == last)
    def _():
        copy_to(ro.at[pl.ds(0, ndp - 1)], ro.at[pl.ds(0, ndp - 1)], ro_send, ro_recv, at(mx, my)).wait_recv()
        forecast(me, True)
        for row in order[1:]:
            forecast(column(0, row))
        for row in order:
            forecast(column(1, row))

    for shift in (-1, 2):
        for row in order:
            wait_block(column(shift, row), 1)

            @pl.when(sec == last)
            def _(shift=shift, row=row):
                forecast(column(shift, row))

    @pl.when(sec == last)
    def _():
        diff = est[...] - gt_ref[...]
        micro = ntok // vl_ref.shape[0]
        offset = lax.broadcasted_iota(jnp.int32, (micro, diff.shape[1]), 0)
        errs = []
        for m in range(vl_ref.shape[0]):
            mask = jnp.where(offset < vl_ref[m], 1.0, 0.0)
            errs.append(mask * diff[m * micro : (m + 1) * micro])
        error = jnp.concatenate(errs, axis=0).astype(BF16)
        for b in range(ndp):
            cols = slice(b * blk, (b + 1) * blk)
            top = matmul_nt(error, ro[b])
            inc[:, :, cols] = top.reshape(nmb, rows, blk).astype(BF16)

    def send_early(j, c):
        p = peer(j)
        copy_to(act.at[me], act.at[me], a_send, a_recv, {"dp": p}).start()
        copy_to(normed.at[p], ncols.at[me], n_send, n_recv, {"dp": p}).start()
        return c

    @pl.when(even & (sec < nsec - TOP))
    def _():
        pl.semaphore_signal(clear, inc=1, device_id={"section": sec + 1}, device_id_type=MESH)

    @pl.when(jnp.logical_not(even) & (sec < nsec - TOP))
    def _():
        pl.semaphore_wait(clear, 1)

    @pl.when(sec < nsec - TOP)
    def _():
        lax.fori_loop(1, ndp, send_early, 0)

    ncols[me] = normed[me]

    below = {"section": (sec + last) % nsec}
    per = ndp // SPLIT

    def relay_copy(m, q):
        cols = slice(q * per * blk, (q + 1) * per * blk)
        return copy_to(outp.at[m, :, cols], inc.at[m, :, cols], r_send.at[m, q], r_recv.at[m, q], below)

    def step(m, c):
        tok = pl.ds(pl.multiple_of(m * rows, rows), rows)
        h = jnp.zeros((rows, latw), F32)
        for q in range(SPLIT):

            @pl.when(sec < last)
            def _(q=q):
                relay_copy(m, q).wait_recv()

            for b in range(q * per, (q + 1) * per):
                h = h + matmul(inc[m, :, b * blk : (b + 1) * blk], wu[b])
        latent_grad = (h * dsil[tok, :]).astype(BF16)
        lg[me, m, :, 0:latw] = latent_grad
        iv = inv[tok, 0:1]
        mean = jnp.sum(latent_grad.astype(F32) * lat[tok, :], axis=-1, keepdims=True) * (1.0 / width)
        lane = lax.broadcasted_iota(jnp.int32, (rows, SIDE), 1)
        lg[me, m, :, latw:] = jnp.where(lane < SIDE // 2, iv, iv * mean).astype(BF16)
        for q in range(SPLIT):
            for b in range(q * per, (q + 1) * per):
                cols = slice(b * blk, (b + 1) * blk)
                scaled = matmul(latent_grad, wd[b]) * gain_ref[:, cols].astype(F32)
                unit = x_ref[m, :, cols].astype(F32) * iv
                g = inc[m, :, cols].astype(F32) + iv * (scaled - unit * mean)
                outp[m, :, cols] = g.astype(BF16)

            @pl.when(sec > 0)
            def _(q=q):
                relay_copy(m, q).start()

        return c

    own_cols = pl.ds(pl.multiple_of(me * blk, blk), blk)

    def send_lg(e, g, dev):
        part = pl.ds(g * GROUP, GROUP)
        copy_to(lg.at[e, part], lg.at[e, part], l_send, l_recv.at[e, g], dev).start()

    def wait_lg(e, g):
        part = pl.ds(g * GROUP, GROUP)
        copy_to(lg.at[e, part], lg.at[e, part], l_send, l_recv.at[e, g], left).wait_recv()

    def pass_on(g):
        @pl.when(g < groups)
        def _():
            send_lg(me, g, left)
            send_lg(me, g, right)
            for row in order[1:]:
                send_lg(me, g, at(mx, row))
        def send_columns():
            part = pl.ds((g + 1 - COT_GROUPS) * GROUP, GROUP * COT_GROUPS)

            def send_cot(j, c):
                p = peer(j)
                p_cols = pl.ds(pl.multiple_of(p * blk, blk), blk)
                copy_to(inc.at[part, :, p_cols], cot.at[me, part], c_send, c_recv, {"dp": p}).start()
                return c

            lax.fori_loop(1, ndp, send_cot, 0)

        @pl.when((g < groups) & (g % COT_GROUPS == COT_GROUPS - 1))
        def _():
            pl.when(odd)(send_columns)

        @pl.when((g >= LAG) & (g < groups + LAG))
        def _():
            for row in order[1:]:
                wait_lg(column(0, row), g - LAG)
                send_lg(column(0, row), g - LAG, left)
                send_lg(column(0, row), g - LAG, right)

        @pl.when(g >= 2 * LAG)
        def _():
            for n, row in enumerate(order):
                near = 1 if n % 2 else -1
                e = column(near, row)
                wait_lg(e, g - 2 * LAG)
                send_lg(e, g - 2 * LAG, left if n % 2 else right)

    groups = nmb // GROUP

    def stretch(g, c):
        lax.fori_loop(g * GROUP, (g + 1) * GROUP, step, 0)
        part = pl.ds(g * GROUP, GROUP)
        pltpu.make_async_copy(outp.at[part], out_ref.at[part], out_sem).start()
        pass_on(g)
        return c

    lax.fori_loop(0, groups, stretch, 0)
    for g in range(groups, groups + 2 * LAG):
        pass_on(g)

    @pl.when(sec >= nsec - TOP)
    def _():
        lax.fori_loop(1, ndp, send_early, 0)

    own = pltpu.make_async_copy(inc.at[:, :, own_cols], cot.at[me], own_sem)

    @pl.when(odd)
    def _():
        own.start()
        own.wait()

    others = pl.ds(0, ndp - 1)
    def last_lg(g, c):
        for n, row in enumerate(order):
            wait_lg(column(-1 if n % 2 else 1, row), g)
            wait_lg(column(2, row), g)
        return c

    lax.fori_loop(0, groups, last_lg, 0)
    copy_to(ncols.at[others], ncols.at[others], n_send, n_recv, at(mx, my)).wait_recv()

    def ship(e):
        return copy_to(cot_next.at[e], cot.at[e], x_send, x_recv, below)

    @pl.when(odd)
    def _():
        copy_to(cot.at[others], cot.at[others], c_send, c_recv, at(mx, my)).wait_recv()
        gain_own = gain_ref[:, own_cols].astype(F32)
        gain_inv = 1.0 / gain_own

        def next_cols(e, c):
            side = lg[e, :, :, latw:].astype(F32).reshape(ntok, SIDE)
            scaled = matmul(flat(lg[e, :, :, 0:latw], ntok), wd[me]) * gain_own
            unit = ncols[e].astype(F32) * gain_inv
            grad = cot[e].astype(F32).reshape(ntok, blk) + side[:, 0:1] * scaled - side[:, SIDE // 2 : SIDE // 2 + 1] * unit
            cot_next[e] = grad.reshape(nmb, rows, blk).astype(BF16)
            ship(e).start()
            return c

        lax.fori_loop(0, ndp, next_cols, 0)

    dg = matmul_tn(ncols[...].reshape(ndp * ntok, blk), flat(lg[:, :, :, 0:latw], ndp * ntok))
    dg_ref[...] = dg.astype(BF16)
    copy_to(act.at[others], act.at[others], a_send, a_recv, at(mx, my)).wait_recv()

    @pl.when(even)
    def _():
        copy_to(cot, cot, x_send, x_recv, below).wait_recv()

    ug = matmul_tn(act[...].reshape(ndp * ntok, latw), flat(cot[...], ndp * ntok))
    ug_ref[...] = ug.astype(BF16)

    pltpu.make_async_copy(outp, out_ref, out_sem).wait()
    for k in (0, 1):
        copy_to(pieces[k].at[others], pieces[k].at[others], w_send, w_recv.at[k, 0], at(mx, my)).wait_send()

    @pl.when(sec == last)
    def _():
        copy_to(ro.at[others], ro.at[others], ro_send, ro_recv, at(mx, my)).wait_send()

    copy_to(act.at[others], act.at[others], a_send, a_recv, at(mx, my)).wait_send()
    copy_to(ncols.at[others], ncols.at[others], n_send, n_recv, at(mx, my)).wait_send()

    @pl.when(odd)
    def _():
        copy_to(cot.at[others], cot.at[others], c_send, c_recv, at(mx, my)).wait_send()
        copy_to(cot_next, cot, x_send, x_recv, below).wait_send()

    copy_to(lg.at[others], lg.at[others], l_send, l_recv.at[0, 0], left).wait_send()

    @pl.when(sec > 0)
    def _():
        def gone(m, c):
            for q in range(SPLIT):
                relay_copy(m, q).wait_send()
            return c

        lax.fori_loop(0, nmb, gone, 0)


def hand_over_kernel(pieces, a_in, b_in, c_in, a_out, b_out, c_out, a_buf, b_buf, c_buf, in_sem, out_sem):
    rows = a_buf.shape[0] // pieces
    jobs = [(b_in, b_buf, b_out), (c_in, c_buf, c_out)]
    for i in range(pieces):
        part = pl.ds(i * rows, rows)
        jobs.append((a_in.at[part], a_buf.at[part], a_out.at[part]))
    for i, (src, buf, _) in enumerate(jobs):
        pltpu.make_async_copy(src, buf, in_sem.at[i]).start()
    for i, (src, buf, dst) in enumerate(jobs):
        pltpu.make_async_copy(src, buf, in_sem.at[i]).wait()
        pltpu.make_async_copy(buf, dst, out_sem.at[i]).start()
    for i, (_, buf, dst) in enumerate(jobs):
        pltpu.make_async_copy(buf, dst, out_sem.at[i]).wait()


def hand_over(*arrays, pieces=4):
    anywhere = pl.BlockSpec(memory_space=pl.ANY)
    return pl.pallas_call(
        functools.partial(hand_over_kernel, pieces),
        name="hand_over",
        out_shape=tuple(jax.ShapeDtypeStruct(a.shape, a.dtype) for a in arrays),
        in_specs=[anywhere] * 3,
        out_specs=(anywhere,) * 3,
        scratch_shapes=[pltpu.VMEM(a.shape, a.dtype) for a in arrays]
        + [pltpu.SemaphoreType.DMA((2 + pieces,)), pltpu.SemaphoreType.DMA((2 + pieces,))],
    )(*arrays)


def per_device(
    ndp, nsec, section_inputs, norm_gain, down_proj, up_proj, readout_matrix, ground_truth_series, valid_len
):
    _, ntok, width = section_inputs.shape
    _, blk, latw = down_proj.shape
    horizon = readout_matrix.shape[1]
    rows = ROWS
    nmb = ntok // rows
    vmem = pl.BlockSpec(memory_space=pltpu.VMEM)
    dma = pltpu.SemaphoreType.DMA
    grads, dg, ug = pl.pallas_call(
        functools.partial(kernel, ndp, nsec),
        name="relay",
        out_shape=(
            jax.ShapeDtypeStruct((nmb, rows, width), BF16),
            jax.ShapeDtypeStruct((blk, latw), BF16),
            jax.ShapeDtypeStruct((latw, blk), BF16),
        ),
        in_specs=[vmem] * 6 + [pl.BlockSpec(memory_space=pltpu.SMEM)],
        out_specs=(pl.BlockSpec(memory_space=pl.ANY), vmem, vmem),
        scratch_shapes=[
            pltpu.VMEM((ndp, latw, blk), BF16),
            pltpu.VMEM((ndp, blk, latw), BF16),
            pltpu.VMEM((ndp, blk, horizon), BF16),
            pltpu.VMEM((ndp, ntok, blk), BF16),
            pltpu.VMEM((ndp, ntok, blk), BF16),
            pltpu.VMEM((ndp, ntok, latw), BF16),
            pltpu.VMEM((ntok, latw), F32),
            pltpu.VMEM((ntok, latw), F32),
            pltpu.VMEM((ntok, 128), F32),
            pltpu.VMEM((nmb, rows, width), BF16),
            pltpu.VMEM((ndp, nmb, rows, latw + SIDE), BF16),
            pltpu.VMEM((ndp, nmb, rows, blk), BF16),
            pltpu.VMEM((nmb, rows, width), BF16),
            pltpu.VMEM((ntok, horizon), F32),
            pltpu.VMEM((ndp, nmb, rows, blk), BF16),
            dma,
            dma((2, ndp)),
            dma,
            dma,
            dma,
            dma,
            dma,
            dma,
            dma,
            dma,
            dma,
            dma((ndp, nmb // GROUP)),
            dma((nmb, SPLIT)),
            dma((nmb, SPLIT)),
            dma,
            dma,
            dma,
            dma,
            pltpu.SemaphoreType.REGULAR,
        ],
        compiler_params=pltpu.CompilerParams(collective_id=0, has_side_effects=True),
    )(
        section_inputs.reshape(nmb, rows, width),
        norm_gain,
        down_proj[0],
        up_proj[0],
        readout_matrix,
        ground_truth_series,
        valid_len,
    )
    grads, dg, ug = hand_over(grads.reshape(ntok, width), dg, ug)
    return grads[None], dg[None], ug[None]


def solution(mesh):
    placed = (
        P("section", "dp", None),
        P("section", None),
        P("section", "dp", None),
        P("section", None, "dp"),
        P("dp", None),
        P("dp", None),
        P("dp"),
    )
    return jax.shard_map(
        functools.partial(per_device, mesh.shape["dp"], mesh.shape["section"]),
        mesh=mesh,
        in_specs=placed,
        out_specs=(P("section", "dp", None), P("section", "dp", None), P("section", None, "dp")),
        check_vma=False,
    )
```
